512 devices in a mesh: stn: 64 (over x, y, z_lo), chan: 8 (over z_hi, core).
Axes of the slice: x: 4, y: 8, z: 8 (z_hi: 4, z_lo: 2; z = z_hi * 2 + z_lo), core: 2. Of those that a mesh axis runs over, the one named last changes fastest.
Arguments:
- voltages: bfloat16 [512, 16, 64, 128], P('stn', 'chan'), may hold values from -12 to 12
- response: bfloat16 [512, 16, 64, 128], P('stn', 'chan'), may hold values from -48 to 48
- start_gains: float32 [512, 128], replicated, may hold values from 0.5 to 1.5
- step_sizes: float32 [64], replicated, may hold values from 0.2 to 0.8
- station_ids: int32 [512], P('stn'), may hold values from 0 to 511, each once
- baseline_flags: int32 [512, 512], replicated, may hold values 0 or 1
Outputs:
- calibrated: float32 [512, 128], P('stn')
- descent: float32 [512, 128], P('stn')
The draws below stay inside these ranges and needn't reach their ends.
Inputs may be any that keep to these rules, and one draw needn't show every extreme that they name: `station_ids`: each station number appears once. `baseline_flags`: 1 keeps a baseline, 0 flags it.
All inputs are finite; a program needn't handle non-finite values.
Results may differ from the reference program's by a relative error of at most 0.0003.
Values may be sent and summed in bfloat16 or wider, within the bound.
No kernel may reach another device: no remote copies, remote signals or barrier semaphores. Data moves between devices by JAX's collectives and lax.ppermute only.
A program may use at most 64 MiB of HBM per device.

```python
import math
import jax
import jax.numpy as jnp
from jax import lax

S = 512
K = 64
NV = 64
TIMES = 64
F = 16
ITERS = 2


def draw_response(key, part):
    keys = jax.random.split(key, 3)
    station_pos = jnp.arange(S, dtype=jnp.float32).reshape(S, 1, 1, 1) / (S - 1)
    station_scale = jnp.exp(jnp.log(3.0) * (station_pos + jax.random.uniform(keys[1], (S, 1, 1, 1), jnp.float32, -0.5, 0.5)))
    direction_scale = jnp.exp(jax.random.uniform(keys[2], (K,), jnp.float32, jnp.log(0.3), jnp.log(3.0)))
    direction_scale = jnp.concatenate([direction_scale, direction_scale]).reshape(1, 1, 1, 2 * K)
    base = jnp.clip(jax.random.normal(keys[0], (S, F, TIMES, 2 * K), jnp.float32), -3.0, 3.0)
    return (base * station_scale * direction_scale).astype(jnp.bfloat16)


def plant(result, rng, smallest, top_value):
    dims = result.shape
    index_at = [jax.random.randint(jax.random.fold_in(rng, axis), (), 0, dims[axis]) for axis in range(len(dims))]
    result = result.at[tuple(index_at)].set(smallest)
    longest = dims.index(max(dims))
    index_at[longest] = (index_at[longest] + 1) % dims[longest]
    return result.at[tuple(index_at)].set(top_value)


def block_scale(own_key, extent, cuts, least, largest):
    factor_of = 1.0
    for dim, blocks in cuts:
        heights = jax.random.uniform(jax.random.fold_in(jax.random.fold_in(own_key, 6), dim), (blocks,), jnp.float32, least / len(cuts), largest / len(cuts))
        factor_of = factor_of * jnp.repeat(jnp.exp(heights), extent[dim] // blocks).reshape((-1,) + (1,) * (len(extent) - 1 - dim))
    return factor_of


def normal_values(rng, shape, deviation, limit, cuts=(), held_as=jnp.bfloat16):
    gain = block_scale(rng, shape, cuts, -0.22, 0.18) if cuts else 1.0
    drawn = jax.random.normal(rng, shape, jnp.float32) * deviation * gain
    return jnp.minimum(jnp.maximum(drawn, -limit), limit).astype(held_as)


def setup_inputs(seed: int = 0) -> dict:
    seeds = jax.random.split(jax.random.key(seed), 7)
    voltages = normal_values(seeds[0], (S, F, TIMES, 2 * NV), 3.0, 12.0, ((0, 64), (1, 8)))
    response = draw_response(jax.random.fold_in(seeds[6], 71), 0)
    start_gains = jnp.clip(1.0 + 0.1 * jax.random.normal(seeds[2], (S, 2 * K), jnp.float32), 0.5, 1.5)
    step_sizes = jnp.clip(jnp.exp(jax.random.uniform(seeds[3], (K,), jnp.float32, math.log(0.2), math.log(0.8))), 0.2, 0.8)
    station_ids = jax.random.permutation(seeds[4], S).astype(jnp.int32)
    baseline_flags = plant((jax.random.randint(seeds[5], (S, S), 0, 8) < 7).astype(jnp.int32), jax.random.fold_in(seeds[5], 1), 0, 1)
    return dict(voltages=voltages, response=response, start_gains=start_gains, step_sizes=step_sizes, station_ids=station_ids, baseline_flags=baseline_flags)


def rotate(values, middle):
    return jnp.concatenate([-values[..., middle:], values[..., :middle]], axis=-1)

def correlate(mine, middle):
    highest = lax.Precision.HIGHEST
    real_part = jnp.einsum('tpc,tqc->tpq', mine, mine, precision=highest)
    imag_part = jnp.einsum('tpc,tqc->tpq', mine, rotate(mine, middle), precision=highest)
    return (real_part / middle, imag_part / middle)

def reference(voltages, response, start_gains, step_sizes, station_ids, baseline_flags):
    highest = lax.Precision.HIGHEST
    samples = F * TIMES
    block = 8
    count = samples // block
    volt_blocks = voltages.astype(jnp.float32).reshape(S, samples, 2 * NV).transpose(1, 0, 2).reshape(count, block, S, 2 * NV)
    resp_blocks = response.astype(jnp.float32).reshape(S, samples, 2 * K).transpose(1, 0, 2).reshape(count, block, S, 2 * K)
    flag_float = baseline_flags.astype(jnp.float32)
    picked = jnp.take(jnp.take(flag_float, station_ids, axis=0), station_ids, axis=1)
    weight = picked * picked.T * (1.0 - jnp.eye(S, dtype=jnp.float32))
    step_both = jnp.concatenate([step_sizes, step_sizes])
    current = start_gains
    descent = jnp.zeros_like(start_gains)
    for iteration in range(ITERS):
        gain_real = current[None, :, :K]
        gain_imag = current[None, :, K:]

        def one_block(total, pieces):
            volts, resp = pieces
            resp_real = resp[..., :K]
            resp_imag = resp[..., K:]
            applied = jnp.concatenate([gain_real * resp_real - gain_imag * resp_imag, gain_real * resp_imag + gain_imag * resp_real], axis=-1).astype(jnp.bfloat16)
            applied_float = lax.optimization_barrier(applied).astype(jnp.float32)
            seen_real, seen_imag = correlate(volts, NV)
            pred_real, pred_imag = correlate(applied_float, K)
            resid_real = (weight[None] * (seen_real - pred_real)).astype(jnp.bfloat16)
            resid_imag = (weight[None] * (seen_imag - pred_imag)).astype(jnp.bfloat16)
            resid_real = lax.optimization_barrier(resid_real).astype(jnp.float32)
            resid_imag = lax.optimization_barrier(resid_imag).astype(jnp.float32)
            hidden = jnp.einsum('tpq,tqc->tpc', resid_real, applied_float, precision=highest)
            hidden = hidden + jnp.einsum('tpq,tqc->tpc', resid_imag, rotate(applied_float, K), precision=highest)
            energy_real = lax.optimization_barrier(jnp.sum(resp_real * hidden[..., :K] + resp_imag * hidden[..., K:], axis=0))
            energy_imag = lax.optimization_barrier(jnp.sum(resp_real * hidden[..., K:] - resp_imag * hidden[..., :K], axis=0))
            return (total + jnp.concatenate([energy_real, energy_imag], axis=-1), None)
        energy, unused = lax.scan(one_block, jnp.zeros((S, 2 * K), jnp.float32), (volt_blocks, resp_blocks))
        gradient = -(2.0 / K) * energy
        spread = jnp.sqrt(jnp.sum(gradient * gradient) / (S * K) + 1e-06)
        descent = gradient / spread
        current = current - step_both[None, :] * descent
    return (current, descent)
```

```python
import functools

import jax
import jax.numpy as jnp
from jax import lax
from jax.experimental import pallas as pl
from jax.experimental.pallas import tpu as pltpu
from jax.sharding import PartitionSpec as P

LIMIT = 48 * 1024 * 1024
f32 = jnp.float32
bf16 = jnp.bfloat16


def call(body, outs, args, name, smem=(), alias=None):
    specs = [
        pl.BlockSpec(memory_space=pltpu.SMEM if i in smem else pltpu.VMEM) for i in range(len(args))
    ]
    single = not isinstance(outs, (tuple, list))
    listed = [outs] if single else list(outs)
    result = pl.pallas_call(
        body,
        out_shape=listed,
        in_specs=specs,
        out_specs=[pl.BlockSpec(memory_space=pltpu.VMEM) for _ in listed],
        compiler_params=pltpu.CompilerParams(vmem_limit_bytes=LIMIT),
        name=name,
    )(*args)
    return result[0] if single else result


def lanes(shape):
    return lax.broadcasted_iota(jnp.int32, shape, len(shape) - 1)


def swap(values):
    half = values.shape[-1] // 2
    return pltpu.roll(values, half, values.ndim - 1)


def rotate(values):
    half = values.shape[-1] // 2
    turned = swap(values)
    return jnp.where(lanes(values.shape) < half, -turned, turned)


def pack_body(ids_ref, volt_ref, resp_ref, out_ref):
    stations, bands = volt_ref.shape[0], volt_ref.shape[1]
    targets = out_ref.shape[0]
    for slot, ref in ((0, volt_ref), (bands, resp_ref)):
        for band in range(bands):
            piece = ref[:, band].astype(f32)
            out_ref[:, slot + band] = jnp.transpose(piece, (1, 0, 2)).astype(bf16)
    row = lax.broadcasted_iota(jnp.int32, (stations, out_ref.shape[3]), 0)
    number = jnp.zeros(row.shape, f32)
    for station in range(stations):
        number = jnp.where(row == station, (ids_ref[station] - 256).astype(f32), number)
    out_ref[:, 2 * bands] = jnp.broadcast_to(number[None], (targets,) + number.shape).astype(bf16)


def both_body(flag_ref, out_ref):
    flags = flag_ref[...].astype(f32)
    out_ref[...] = (flags * flags.T).astype(bf16)


def dot_nt(left, right):
    return lax.dot_general(left, right, (((1,), (1,)), ((), ())), preferred_element_type=f32)


def weigh(number, both):
    everyone, width = number.shape
    pieces = [
        number == (lanes(number.shape) + (piece * width - 256)).astype(f32)
        for piece in range(everyone // width)
    ]
    chosen = jnp.concatenate([jnp.where(p, 1.0, 0.0).astype(bf16) for p in pieces], axis=1)
    half = jnp.dot(chosen, both, preferred_element_type=f32).astype(bf16)
    picked = dot_nt(half, chosen)
    rows = lax.broadcasted_iota(jnp.int32, picked.shape, 0)
    return jnp.where(rows == lanes(picked.shape), 0.0, picked * (1.0 / 64.0))


def energy_of(volts, resps, gains, weight_ref, out_ref, rows):
    everyone, width = gains.shape
    half = width // 2
    low = lanes(gains.shape) < half
    turned = swap(gains)
    straight = jnp.where(low, gains, turned)
    crossed = jnp.where(low, -turned, gains)
    lefts, rights, backs = [], [], []
    for volt, resp in zip(volts, resps):
        applied = (straight * resp + crossed * swap(resp)).astype(bf16)
        applied_float = applied.astype(f32)
        turned_applied = rotate(applied_float).astype(bf16)
        volt_low = volt.astype(bf16)
        lefts.append(jnp.concatenate([volt_low, (-applied_float).astype(bf16)], axis=1))
        rights.append(
            jnp.concatenate(
                [
                    jnp.concatenate([volt_low, applied], axis=1),
                    jnp.concatenate([rotate(volt).astype(bf16), turned_applied], axis=1),
                ],
                axis=0,
            )
        )
        backs.append(jnp.concatenate([applied, turned_applied], axis=0))
    for start in range(0, everyone, rows):
        weight = weight_ref[start : start + rows]
        weight_both = jnp.concatenate([weight, weight], axis=1)
        same = cross = 0.0
        for left, right, back, resp in zip(lefts, rights, backs, resps):
            short = dot_nt(left[start : start + rows], right)
            residual = (weight_both * short).astype(bf16)
            hidden = jnp.dot(residual, back, preferred_element_type=f32)
            part = resp[start : start + rows]
            same = same + part * hidden
            cross = cross + part * swap(hidden)
        real = same + swap(same)
        imag = swap(cross) - cross
        out_ref[start : start + rows] = jnp.where(lanes(real.shape) < half, real, imag)


def slabs(data_ref, first, count):
    everyone = data_ref.shape[0] * data_ref.shape[2]
    return [
        data_ref[:, first + i].astype(f32).reshape(everyone, data_ref.shape[3])
        for i in range(count)
    ]


def first_body(bands, rows, data_ref, both_ref, gain_ref, out_ref, weight_ref):
    weight_ref[...] = weigh(slabs(data_ref, 2 * bands, 1)[0], both_ref[...])
    energy_of(
        slabs(data_ref, 0, bands),
        slabs(data_ref, bands, bands),
        gain_ref[...],
        weight_ref,
        out_ref,
        rows,
    )


def next_body(bands, rows, stations, at_ref, total_ref, step_ref, gain_ref, data_ref, weight_ref, out_ref, own_ref):
    everyone, width = gain_ref.shape
    gradient = total_ref[...].reshape(everyone, width) * (-4.0 / width)
    square = jnp.sum(jnp.sum(gradient * gradient, axis=0, keepdims=True), axis=1, keepdims=True)
    scale = 1.0 / jnp.sqrt(square * (2.0 / (everyone * width)) + 1e-06)
    gains = gain_ref[...] - step_ref[...] * (gradient * scale)
    weight_at = at_ref[0] * stations
    out_ref[...] = gains
    own_ref[...] = out_ref[pl.ds(pl.multiple_of(weight_at, stations), stations)]
    energy_of(slabs(data_ref, 0, bands), slabs(data_ref, bands, bands), gains, weight_ref, out_ref, rows)


def spread_out_body(in_ref, out_ref):
    out_ref[...] = jnp.broadcast_to(jnp.sum(in_ref[...], axis=0)[None], out_ref.shape)


def square_body(in_ref, grad_ref, out_ref):
    width = in_ref.shape[2]
    gradient = jnp.sum(in_ref[...], axis=0) * (-4.0 / width)
    grad_ref[...] = gradient
    square = jnp.sum(gradient * gradient, axis=0, keepdims=True)
    out_ref[...] = jnp.broadcast_to(square[None], out_ref.shape)


def last_body(everyone, square_ref, grad_ref, gain_ref, step_ref, out_ref, descent_ref):
    width = grad_ref.shape[1]
    square = jnp.sum(jnp.sum(square_ref[...], axis=0), axis=1, keepdims=True)
    descent = grad_ref[...] * (1.0 / jnp.sqrt(square * (2.0 / (everyone * width)) + 1e-06))
    descent_ref[...] = descent
    out_ref[...] = gain_ref[...] - step_ref[...] * descent


def shards(voltages, response, start_gains, step_sizes, station_ids, baseline_flags):
    stations, bands, times, width = voltages.shape
    ring = lax.axis_size("stn")
    deep = lax.axis_size("chan")
    everyone = stations * ring
    rows = 256
    shape = jax.ShapeDtypeStruct
    step_both = jnp.concatenate([step_sizes, step_sizes])[None, :]
    at = lax.axis_index("stn").reshape(1)

    def swap_over(values, axis):
        return lax.all_to_all(values, axis, split_axis=0, concat_axis=0, tiled=True)

    packed = call(
        pack_body,
        shape((ring, 2 * bands + 1, stations, width), bf16),
        (station_ids, voltages, response),
        "pack",
        smem=(0,),
    )
    data = swap_over(packed, "stn")
    both = call(both_body, shape((everyone, everyone), bf16), (baseline_flags,), "both")
    energy, weight = call(
        functools.partial(first_body, bands, rows),
        (shape((everyone, width), f32), shape((everyone, everyone), f32)),
        (data, both, start_gains),
        "first",
    )

    def reduced(energy):
        parts = swap_over(energy.reshape(ring, stations, width), "stn")
        copies = call(spread_out_body, shape((deep, stations, width), f32), (parts,), "sum_stn")
        return swap_over(copies, "chan")

    copies = call(spread_out_body, shape((ring, stations, width), f32), (reduced(energy),), "sum_chan")
    total = swap_over(copies, "stn")
    energy, own = call(
        functools.partial(next_body, bands, rows, stations),
        (shape((everyone, width), f32), shape((stations, width), f32)),
        (at, total, step_both, start_gains, data, weight),
        "next",
        smem=(0,),
    )
    gradient, square = call(
        square_body,
        (shape((stations, width), f32), shape((ring, 1, width), f32)),
        (reduced(energy),),
        "square",
    )
    squares = swap_over(square, "stn")
    return call(
        functools.partial(last_body, everyone),
        (shape((stations, width), f32), shape((stations, width), f32)),
        (squares, gradient, own, step_both),
        "last",
    )


def solution(mesh):
    placed = (P("stn", "chan", None, None), P("stn", "chan", None, None), P(), P(), P("stn"), P())
    return jax.shard_map(
        shards,
        mesh=mesh,
        in_specs=placed,
        out_specs=(P("stn", None), P("stn", None)),
        check_vma=False,
    )
```

```python
import functools

import jax
import jax.numpy as jnp
from jax import lax
from jax.experimental import pallas as pl
from jax.experimental.pallas import tpu as pltpu
from jax.sharding import Mesh
from jax.sharding import PartitionSpec as P

LIMIT = 48 * 1024 * 1024
f32 = jnp.float32
bf16 = jnp.bfloat16


def call(body, outs, args, name, smem=(), left=(), scratch=()):
    specs = [
        pl.BlockSpec(memory_space=pltpu.SMEM if i in smem else pltpu.HBM if i in left else pltpu.VMEM)
        for i in range(len(args))
    ]
    single = not isinstance(outs, (tuple, list))
    listed = [outs] if single else list(outs)
    result = pl.pallas_call(
        body,
        out_shape=listed,
        in_specs=specs,
        out_specs=[pl.BlockSpec(memory_space=pltpu.VMEM) for _ in listed],
        scratch_shapes=list(scratch),
        compiler_params=pltpu.CompilerParams(vmem_limit_bytes=LIMIT),
        name=name,
    )(*args)
    return result[0] if single else result


def lanes(shape):
    return lax.broadcasted_iota(jnp.int32, shape, len(shape) - 1)


def swap(values):
    half = values.shape[-1] // 2
    return pltpu.roll(values, half, values.ndim - 1)


def rotate(values):
    half = values.shape[-1] // 2
    turned = swap(values)
    return jnp.where(lanes(values.shape) < half, -turned, turned)


def pack_body(volt_ref, resp_ref, out_ref, held, sems):
    bands = held.shape[0] // 2
    copies = [
        pltpu.make_async_copy(ref.at[:, band], held.at[slot + band], sems.at[slot + band])
        for slot, ref in ((0, volt_ref), (bands, resp_ref))
        for band in range(bands)
    ]
    for copy in copies:
        copy.start()
    for slot, copy in enumerate(copies):
        copy.wait()
        out_ref[:, slot] = jnp.transpose(held[slot].astype(f32), (1, 0, 2)).astype(bf16)


def both_body(flag_ref, out_ref):
    flags = flag_ref[...].astype(f32)
    out_ref[...] = (flags * flags.T).astype(bf16)


def dot_nt(left, right):
    return lax.dot_general(left, right, (((1,), (1,)), ((), ())), preferred_element_type=f32)


def weigh_body(stations, at_ref, number_ref, both_ref, gain_ref, step_ref, out_ref, own_ref, wide_ref):
    everyone = both_ref.shape[0]
    width = gain_ref.shape[1]
    rows = lax.broadcasted_iota(jnp.int32, (everyone, width), 0)
    pieces = [
        jnp.where(rows == number_ref[pl.ds(start, width)][None, :], 1.0, 0.0).astype(bf16)
        for start in range(0, everyone, width)
    ]
    chosen = jnp.concatenate(pieces, axis=1)
    half = jnp.dot(both_ref[...], chosen, preferred_element_type=f32).astype(bf16)
    picked = lax.dot_general(chosen, half, (((0,), (0,)), ((), ())), preferred_element_type=f32)
    rows = lax.broadcasted_iota(jnp.int32, picked.shape, 0)
    out_ref[...] = jnp.where(rows == lanes(picked.shape), 0.0, picked * (1.0 / 64.0))
    own_ref[...] = gain_ref[pl.ds(pl.multiple_of(at_ref[0] * stations, stations), stations)]
    wide_ref[...] = jnp.concatenate([step_ref[...], step_ref[...]], axis=1)


def energy_of(volts, resps, gains, weight_ref, out_ref, rows):
    everyone, width = gains.shape
    half = width // 2
    low = lanes(gains.shape) < half
    turned = swap(gains)
    straight = jnp.where(low, gains, turned)
    crossed = jnp.where(low, -turned, gains)
    lefts, rights, backs = [], [], []
    for volt, resp in zip(volts, resps):
        applied = (straight * resp + crossed * swap(resp)).astype(bf16)
        applied_float = applied.astype(f32)
        turned_applied = rotate(applied_float).astype(bf16)
        volt_low = volt.astype(bf16)
        lefts.append(jnp.concatenate([volt_low, (-applied_float).astype(bf16)], axis=1))
        rights.append(
            jnp.concatenate(
                [
                    jnp.concatenate([volt_low, applied], axis=1),
                    jnp.concatenate([rotate(volt).astype(bf16), turned_applied], axis=1),
                ],
                axis=0,
            )
        )
        backs.append(jnp.concatenate([applied, turned_applied], axis=0))
    for start in range(0, everyone, rows):
        weight = weight_ref[start : start + rows]
        weight_both = jnp.concatenate([weight, weight], axis=1)
        same = cross = 0.0
        for left, right, back, resp in zip(lefts, rights, backs, resps):
            short = dot_nt(left[start : start + rows], right)
            residual = (weight_both * short).astype(bf16)
            hidden = jnp.dot(residual, back, preferred_element_type=f32)
            part = resp[start : start + rows]
            same = same + part * hidden
            cross = cross + part * swap(hidden)
        real = same + swap(same)
        imag = swap(cross) - cross
        out_ref[start : start + rows] = jnp.where(lanes(real.shape) < half, real, imag)


def slabs(data_ref, first, count):
    everyone = data_ref.shape[0] * data_ref.shape[2]
    return [
        data_ref[:, first + i].astype(f32).reshape(everyone, data_ref.shape[3])
        for i in range(count)
    ]


def first_body(bands, rows, data_ref, weight_ref, gain_ref, out_ref):
    energy_of(
        slabs(data_ref, 0, bands),
        slabs(data_ref, bands, bands),
        gain_ref[...],
        weight_ref,
        out_ref,
        rows,
    )


def next_body(bands, rows, total_ref, step_ref, gain_ref, data_ref, weight_ref, out_ref, scale_ref):
    everyone, width = gain_ref.shape
    gradient = total_ref[...].reshape(everyone, width) * (-4.0 / width)
    square = jnp.sum(jnp.sum(gradient * gradient, axis=0, keepdims=True), axis=1, keepdims=True)
    scale = 1.0 / jnp.sqrt(square * (2.0 / (everyone * width)) + 1e-06)
    scale_ref[...] = jnp.broadcast_to(scale, scale_ref.shape)
    gains = gain_ref[...] - step_ref[...] * (gradient * scale)
    energy_of(slabs(data_ref, 0, bands), slabs(data_ref, bands, bands), gains, weight_ref, out_ref, rows)


def sum_body(in_ref, out_ref, grad_ref):
    total = jnp.sum(in_ref[...], axis=0)
    out_ref[...] = jnp.broadcast_to(total[None], out_ref.shape)
    grad_ref[...] = total * (-4.0 / in_ref.shape[2])


def split_out_body(in_ref, out_ref):
    blocks, stations = 2, out_ref.shape[1]
    total = jnp.sum(in_ref[...], axis=0)
    each = out_ref.shape[0] // blocks
    for block in range(blocks):
        piece = total[block * stations : (block + 1) * stations]
        out_ref[block * each : (block + 1) * each] = jnp.broadcast_to(piece[None], (each,) + piece.shape)


def square_body(in_ref, grad_ref, out_ref):
    width = in_ref.shape[2]
    gradient = jnp.sum(in_ref[...], axis=0) * (-4.0 / width)
    grad_ref[...] = gradient
    square = jnp.sum(gradient * gradient, axis=0, keepdims=True)
    out_ref[...] = jnp.broadcast_to(square[None], out_ref.shape)


def last_body(everyone, square_ref, grad_ref, gain_ref, step_ref, before_ref, scale_ref, out_ref, descent_ref):
    width = grad_ref.shape[1]
    square = jnp.sum(jnp.sum(square_ref[...], axis=0), axis=1, keepdims=True)
    descent = grad_ref[...] * (1.0 / jnp.sqrt(square * (2.0 / (everyone * width)) + 1e-06))
    gains = gain_ref[...] - step_ref[...] * (before_ref[...] * scale_ref[...])
    descent_ref[...] = descent
    out_ref[...] = gains - step_ref[...] * descent


def shards(voltages, response, start_gains, step_sizes, station_ids, baseline_flags):
    stations, bands, times, width = voltages.shape
    plane = lax.axis_size("plane")
    ring = plane * lax.axis_size("pair")
    column = lax.axis_size("pair") * lax.axis_size("chan")
    stn = ("plane", "pair")
    everyone = stations * ring
    rows = 256
    shape = jax.ShapeDtypeStruct
    step = step_sizes[None, :]
    at = lax.axis_index(stn).reshape(1)

    def swap_over(values, axis):
        return lax.all_to_all(values, axis, split_axis=0, concat_axis=0, tiled=True)

    packed = call(
        pack_body,
        shape((ring, 2 * bands, stations, width), bf16),
        tuple(pltpu.with_memory_space_constraint(a, pltpu.HBM) for a in (voltages, response)),
        "pack",
        left=(0, 1),
        scratch=(
            pltpu.VMEM((2 * bands, stations, times, width), bf16),
            pltpu.SemaphoreType.DMA((2 * bands,)),
        ),
    )
    data = swap_over(packed, stn)
    both = call(both_body, shape((everyone, everyone), bf16), (baseline_flags,), "both")
    placed = lax.dynamic_update_slice(
        jnp.zeros((everyone,), jnp.int32), station_ids, (lax.axis_index(stn) * stations,)
    )
    number = lax.psum(placed, stn)
    weight, own, wide = call(
        functools.partial(weigh_body, stations),
        (shape((everyone, everyone), f32), shape((stations, width), f32), shape((1, width), f32)),
        (at, number, both, start_gains, step),
        "weigh",
        smem=(0,),
    )
    energy = call(
        functools.partial(first_body, bands, rows),
        shape((everyone, width), f32),
        (data, weight, start_gains),
        "first",
    )

    def reduced(energy):
        parts = swap_over(energy.reshape(plane, everyone // plane, width), "plane")
        copies = call(split_out_body, shape((column, stations, width), f32), (parts,), "split")
        return swap_over(copies, ("pair", "chan"))

    copies, before = call(
        sum_body,
        (shape((ring, stations, width), f32), shape((stations, width), f32)),
        (reduced(energy),),
        "sum",
    )
    total = swap_over(copies, stn)
    energy, scale = call(
        functools.partial(next_body, bands, rows),
        (shape((everyone, width), f32), shape((1, width), f32)),
        (total, wide, start_gains, data, weight),
        "next",
    )
    gradient, square = call(
        square_body,
        (shape((stations, width), f32), shape((ring, 1, width), f32)),
        (reduced(energy),),
        "square",
    )
    squares = swap_over(square, stn)
    return call(
        functools.partial(last_body, everyone),
        (shape((stations, width), f32), shape((stations, width), f32)),
        (squares, gradient, own, wide, before, scale),
        "last",
    )


def solution(mesh):
    pair = 2
    devices = mesh.devices
    finer = Mesh(
        devices.reshape(devices.shape[0] // pair, pair, devices.shape[1]), ("plane", "pair", "chan")
    )
    stn = ("plane", "pair")
    placed = (P(stn, "chan", None, None), P(stn, "chan", None, None), P(), P(), P(stn), P())
    return jax.shard_map(
        shards,
        mesh=finer,
        in_specs=placed,
        out_specs=(P(stn, None), P(stn, None)),
        check_vma=False,
    )
```

```python
import functools

import jax
import jax.numpy as jnp
from jax import lax
from jax.experimental import pallas as pl
from jax.experimental.pallas import tpu as pltpu
from jax.sharding import Mesh
from jax.sharding import PartitionSpec as P

LIMIT = 48 * 1024 * 1024
f32 = jnp.float32
bf16 = jnp.bfloat16


def call(body, outs, args, name, smem=(), left=(), scratch=()):
    specs = [
        pl.BlockSpec(memory_space=pltpu.SMEM if i in smem else pltpu.HBM if i in left else pltpu.VMEM)
        for i in range(len(args))
    ]
    single = not isinstance(outs, (tuple, list))
    listed = [outs] if single else list(outs)
    result = pl.pallas_call(
        body,
        out_shape=listed,
        in_specs=specs,
        out_specs=[pl.BlockSpec(memory_space=pltpu.VMEM) for _ in listed],
        scratch_shapes=list(scratch),
        compiler_params=pltpu.CompilerParams(vmem_limit_bytes=LIMIT),
        name=name,
    )(*args)
    return result[0] if single else result


def lanes(shape):
    return lax.broadcasted_iota(jnp.int32, shape, len(shape) - 1)


def swap(values):
    half = values.shape[-1] // 2
    return pltpu.roll(values, half, values.ndim - 1)


def rotate(values):
    half = values.shape[-1] // 2
    turned = swap(values)
    return jnp.where(lanes(values.shape) < half, -turned, turned)


def pack_body(from_ref, volt_ref, resp_ref, out_ref, ids_ref, held, sems):
    bands = held.shape[0] // 2
    copies = [
        pltpu.make_async_copy(ref.at[:, band], held.at[slot + band], sems.at[slot + band])
        for slot, ref in ((0, volt_ref), (bands, resp_ref))
        for band in range(bands)
    ]
    listed = pltpu.make_async_copy(from_ref, ids_ref, sems.at[2 * bands])
    listed.start()
    for copy in copies:
        copy.start()
    listed.wait()
    row = lax.broadcasted_iota(jnp.int32, out_ref.shape[2:], 0)
    number = jnp.zeros(row.shape, f32)
    for station in range(held.shape[1]):
        number = jnp.where(row == station, (ids_ref[station] - 256).astype(f32), number)
    out_ref[:, 2 * bands] = jnp.broadcast_to(number[None], (out_ref.shape[0],) + row.shape).astype(bf16)
    for slot, copy in enumerate(copies):
        copy.wait()
        out_ref[:, slot] = jnp.transpose(held[slot].astype(f32), (1, 0, 2)).astype(bf16)


def dot_nt(left, right):
    return lax.dot_general(left, right, (((1,), (1,)), ((), ())), preferred_element_type=f32)


def ready_body(stations, at_ref, flag_ref, gain_ref, step_ref, both_ref, own_ref, wide_ref):
    flags = flag_ref[...].astype(f32)
    both_ref[...] = (flags * flags.T).astype(bf16)
    own_ref[...] = gain_ref[pl.ds(pl.multiple_of(at_ref[0] * stations, stations), stations)]
    wide_ref[...] = jnp.concatenate([step_ref[...], step_ref[...]], axis=1)


def weigh(number, both):
    everyone, width = number.shape
    pieces = [
        number == (lanes(number.shape) + (piece * width - 256)).astype(f32)
        for piece in range(everyone // width)
    ]
    chosen = jnp.concatenate([jnp.where(p, 1.0, 0.0).astype(bf16) for p in pieces], axis=1)
    half = jnp.dot(chosen, both, preferred_element_type=f32).astype(bf16)
    picked = dot_nt(half, chosen)
    rows = lax.broadcasted_iota(jnp.int32, picked.shape, 0)
    return jnp.where(rows == lanes(picked.shape), 0.0, picked * (1.0 / 64.0))


def energy_of(volts, resps, gains, weight_ref, out_ref, rows):
    everyone, width = gains.shape
    half = width // 2
    low = lanes(gains.shape) < half
    turned = swap(gains)
    straight = jnp.where(low, gains, turned)
    crossed = jnp.where(low, -turned, gains)
    lefts, rights, backs = [], [], []
    for volt, resp in zip(volts, resps):
        applied = (straight * resp + crossed * swap(resp)).astype(bf16)
        applied_float = applied.astype(f32)
        turned_applied = rotate(applied_float).astype(bf16)
        volt_low = volt.astype(bf16)
        lefts.append(jnp.concatenate([volt_low, (-applied_float).astype(bf16)], axis=1))
        rights.append(
            jnp.concatenate(
                [
                    jnp.concatenate([volt_low, applied], axis=1),
                    jnp.concatenate([rotate(volt).astype(bf16), turned_applied], axis=1),
                ],
                axis=0,
            )
        )
        backs.append(jnp.concatenate([applied, turned_applied], axis=0))
    for start in range(0, everyone, rows):
        weight = weight_ref[start : start + rows]
        weight_both = jnp.concatenate([weight, weight], axis=1)
        same = cross = 0.0
        for left, right, back, resp in zip(lefts, rights, backs, resps):
            short = dot_nt(left[start : start + rows], right)
            residual = (weight_both * short).astype(bf16)
            hidden = jnp.dot(residual, back, preferred_element_type=f32)
            part = resp[start : start + rows]
            same = same + part * hidden
            cross = cross + part * swap(hidden)
        real = same + swap(same)
        imag = swap(cross) - cross
        out_ref[start : start + rows] = jnp.where(lanes(real.shape) < half, real, imag)


def slabs(data_ref, first, count):
    everyone = data_ref.shape[0] * data_ref.shape[2]
    return [
        data_ref[:, first + i].astype(f32).reshape(everyone, data_ref.shape[3])
        for i in range(count)
    ]


def first_body(bands, rows, data_ref, both_ref, gain_ref, out_ref, weight_ref):
    weight_ref[...] = weigh(slabs(data_ref, 2 * bands, 1)[0], both_ref[...])
    energy_of(
        slabs(data_ref, 0, bands),
        slabs(data_ref, bands, bands),
        gain_ref[...],
        weight_ref,
        out_ref,
        rows,
    )


def next_body(bands, rows, total_ref, step_ref, gain_ref, data_ref, weight_ref, out_ref, scale_ref):
    everyone, width = gain_ref.shape
    gradient = total_ref[...].reshape(everyone, width) * (-4.0 / width)
    square = jnp.sum(jnp.sum(gradient * gradient, axis=0, keepdims=True), axis=1, keepdims=True)
    scale = 1.0 / jnp.sqrt(square * (2.0 / (everyone * width)) + 1e-06)
    scale_ref[...] = jnp.broadcast_to(scale, scale_ref.shape)
    gains = gain_ref[...] - step_ref[...] * (gradient * scale)
    energy_of(slabs(data_ref, 0, bands), slabs(data_ref, bands, bands), gains, weight_ref, out_ref, rows)


def sum_body(in_ref, out_ref, grad_ref):
    total = jnp.sum(in_ref[...], axis=0)
    out_ref[...] = jnp.broadcast_to(total[None], out_ref.shape)
    grad_ref[...] = total * (-4.0 / in_ref.shape[2])


def split_out_body(in_ref, out_ref):
    blocks, stations = 2, out_ref.shape[1]
    total = jnp.sum(in_ref[...], axis=0)
    each = out_ref.shape[0] // blocks
    for block in range(blocks):
        piece = total[block * stations : (block + 1) * stations]
        out_ref[block * each : (block + 1) * each] = jnp.broadcast_to(piece[None], (each,) + piece.shape)


def square_body(in_ref, grad_ref, out_ref):
    width = in_ref.shape[2]
    gradient = jnp.sum(in_ref[...], axis=0) * (-4.0 / width)
    grad_ref[...] = gradient
    square = jnp.sum(gradient * gradient, axis=0, keepdims=True)
    out_ref[...] = jnp.broadcast_to(square[None], out_ref.shape)


def last_body(everyone, square_ref, grad_ref, gain_ref, step_ref, before_ref, scale_ref, out_ref, descent_ref):
    width = grad_ref.shape[1]
    square = jnp.sum(jnp.sum(square_ref[...], axis=0), axis=1, keepdims=True)
    descent = grad_ref[...] * (1.0 / jnp.sqrt(square * (2.0 / (everyone * width)) + 1e-06))
    gains = gain_ref[...] - step_ref[...] * (before_ref[...] * scale_ref[...])
    descent_ref[...] = descent
    out_ref[...] = gains - step_ref[...] * descent


def shards(voltages, response, start_gains, step_sizes, station_ids, baseline_flags):
    stations, bands, times, width = voltages.shape
    plane = lax.axis_size("plane")
    ring = plane * lax.axis_size("pair")
    column = lax.axis_size("pair") * lax.axis_size("chan")
    stn = ("plane", "pair")
    everyone = stations * ring
    rows = 256
    shape = jax.ShapeDtypeStruct
    step = step_sizes[None, :]
    at = lax.axis_index(stn).reshape(1)

    def swap_over(values, axis):
        return lax.all_to_all(values, axis, split_axis=0, concat_axis=0, tiled=True)

    packed = call(
        pack_body,
        shape((ring, 2 * bands + 1, stations, width), bf16),
        tuple(
            pltpu.with_memory_space_constraint(a, pltpu.HBM)
            for a in (station_ids, voltages, response)
        ),
        "pack",
        left=(0, 1, 2),
        scratch=(
            pltpu.SMEM((stations,), jnp.int32),
            pltpu.VMEM((2 * bands, stations, times, width), bf16),
            pltpu.SemaphoreType.DMA((2 * bands + 1,)),
        ),
    )
    data = swap_over(packed, stn)
    both, own, wide = call(
        functools.partial(ready_body, stations),
        (shape((everyone, everyone), bf16), shape((stations, width), f32), shape((1, width), f32)),
        (at, baseline_flags, start_gains, step),
        "ready",
        smem=(0,),
    )
    energy, weight = call(
        functools.partial(first_body, bands, rows),
        (shape((everyone, width), f32), shape((everyone, everyone), f32)),
        (data, both, start_gains),
        "first",
    )

    def reduced(energy):
        parts = swap_over(energy.reshape(plane, everyone // plane, width), "plane")
        copies = call(split_out_body, shape((column, stations, width), f32), (parts,), "split")
        return swap_over(copies, ("pair", "chan"))

    copies, before = call(
        sum_body,
        (shape((ring, stations, width), f32), shape((stations, width), f32)),
        (reduced(energy),),
        "sum",
    )
    total = swap_over(copies, stn)
    energy, scale = call(
        functools.partial(next_body, bands, rows),
        (shape((everyone, width), f32), shape((1, width), f32)),
        (total, wide, start_gains, data, weight),
        "next",
    )
    gradient, square = call(
        square_body,
        (shape((stations, width), f32), shape((ring, 1, width), f32)),
        (reduced(energy),),
        "square",
    )
    squares = swap_over(square, stn)
    return call(
        functools.partial(last_body, everyone),
        (shape((stations, width), f32), shape((stations, width), f32)),
        (squares, gradient, own, wide, before, scale),
        "last",
    )


def solution(mesh):
    pair = 2
    devices = mesh.devices
    finer = Mesh(
        devices.reshape(devices.shape[0] // pair, pair, devices.shape[1]), ("plane", "pair", "chan")
    )
    stn = ("plane", "pair")
    placed = (P(stn, "chan", None, None), P(stn, "chan", None, None), P(), P(), P(stn), P())
    return jax.shard_map(
        shards,
        mesh=finer,
        in_specs=placed,
        out_specs=(P(stn, None), P(stn, None)),
        check_vma=False,
    )
```

```python
import functools

import jax
import jax.numpy as jnp
import numpy as np
from jax import lax
from jax.experimental import pallas as pl
from jax.experimental.pallas import tpu as pltpu
from jax.sharding import Mesh
from jax.sharding import PartitionSpec as P

LIMIT = 48 * 1024 * 1024
STN = ("x1", "x0", "y2", "y1", "y0", "pair")
ROUND = ("y2", "x1", "y1", "pair", "y0", "x0")
PLANE = ("y2", "x1", "y1", "y0", "x0")
COLUMN = ("pair", "chan")


def numbered(axes):
    whole = np.arange(2 ** len(STN)).reshape((2,) * len(STN))
    return whole.transpose([STN.index(axis) for axis in axes]).reshape(-1)


HELD = [int(number) for number in numbered(ROUND)]
SENT = [int(place) for place in np.argsort(numbered(PLANE + ("pair",)))[numbered(ROUND)]]
f32 = jnp.float32
bf16 = jnp.bfloat16


def call(body, outs, args, name, smem=(), left=(), scratch=()):
    specs = [
        pl.BlockSpec(memory_space=pltpu.SMEM if i in smem else pltpu.HBM if i in left else pltpu.VMEM)
        for i in range(len(args))
    ]
    single = not isinstance(outs, (tuple, list))
    listed = [outs] if single else list(outs)
    result = pl.pallas_call(
        body,
        out_shape=listed,
        in_specs=specs,
        out_specs=[pl.BlockSpec(memory_space=pltpu.VMEM) for _ in listed],
        scratch_shapes=list(scratch),
        compiler_params=pltpu.CompilerParams(vmem_limit_bytes=LIMIT),
        name=name,
    )(*args)
    return result[0] if single else result


def lanes(shape):
    return lax.broadcasted_iota(jnp.int32, shape, len(shape) - 1)


def swap(values):
    half = values.shape[-1] // 2
    return pltpu.roll(values, half, values.ndim - 1)


def rotate(values):
    half = values.shape[-1] // 2
    turned = swap(values)
    return jnp.where(lanes(values.shape) < half, -turned, turned)


def pack_body(from_ref, volt_ref, resp_ref, out_ref, ids_ref, held, sems):
    bands = held.shape[0] // 2
    copies = [
        pltpu.make_async_copy(ref.at[:, band], held.at[slot + band], sems.at[slot + band])
        for slot, ref in ((0, volt_ref), (bands, resp_ref))
        for band in range(bands)
    ]
    listed = pltpu.make_async_copy(from_ref, ids_ref, sems.at[2 * bands])
    listed.start()
    for copy in copies:
        copy.start()
    listed.wait()
    row = lax.broadcasted_iota(jnp.int32, out_ref.shape[2:], 0)
    number = jnp.zeros(row.shape, f32)
    for station in range(held.shape[1]):
        number = jnp.where(row == station, (ids_ref[station] - 256).astype(f32), number)
    out_ref[:, 2 * bands] = jnp.broadcast_to(number[None], (out_ref.shape[0],) + row.shape).astype(bf16)
    for slot, copy in enumerate(copies):
        copy.wait()
        out_ref[:, slot] = jnp.transpose(held[slot].astype(f32), (1, 0, 2)).astype(bf16)


def dot_nt(left, right):
    return lax.dot_general(left, right, (((1,), (1,)), ((), ())), preferred_element_type=f32)


def ready_body(stations, at_ref, flag_ref, gain_ref, step_ref, both_ref, own_ref, wide_ref, held_ref):
    for place, number in enumerate(HELD):
        held_ref[place * stations : (place + 1) * stations] = gain_ref[
            number * stations : (number + 1) * stations
        ]
    flags = flag_ref[...].astype(f32)
    both_ref[...] = (flags * flags.T).astype(bf16)
    own_ref[...] = gain_ref[pl.ds(pl.multiple_of(at_ref[0] * stations, stations), stations)]
    wide_ref[...] = jnp.concatenate([step_ref[...], step_ref[...]], axis=1)


def weigh(number, both):
    everyone, width = number.shape
    pieces = [
        number == (lanes(number.shape) + (piece * width - 256)).astype(f32)
        for piece in range(everyone // width)
    ]
    chosen = jnp.concatenate([jnp.where(p, 1.0, 0.0).astype(bf16) for p in pieces], axis=1)
    half = jnp.dot(chosen, both, preferred_element_type=f32).astype(bf16)
    picked = dot_nt(half, chosen)
    rows = lax.broadcasted_iota(jnp.int32, picked.shape, 0)
    return jnp.where(rows == lanes(picked.shape), 0.0, picked * (1.0 / 64.0))


def energy_of(volts, resps, gains, weight_ref, out_ref, rows):
    everyone, width = gains.shape
    half = width // 2
    low = lanes(gains.shape) < half
    turned = swap(gains)
    straight = jnp.where(low, gains, turned)
    crossed = jnp.where(low, -turned, gains)
    lefts, rights, backs = [], [], []
    for volt, resp in zip(volts, resps):
        applied = (straight * resp + crossed * swap(resp)).astype(bf16)
        applied_float = applied.astype(f32)
        turned_applied = rotate(applied_float).astype(bf16)
        volt_low = volt.astype(bf16)
        lefts.append(jnp.concatenate([volt_low, (-applied_float).astype(bf16)], axis=1))
        rights.append(
            jnp.concatenate(
                [
                    jnp.concatenate([volt_low, applied], axis=1),
                    jnp.concatenate([rotate(volt).astype(bf16), turned_applied], axis=1),
                ],
                axis=0,
            )
        )
        backs.append(jnp.concatenate([applied, turned_applied], axis=0))
    for start in range(0, everyone, rows):
        weight = weight_ref[start : start + rows]
        weight_both = jnp.concatenate([weight, weight], axis=1)
        same = cross = 0.0
        for left, right, back, resp in zip(lefts, rights, backs, resps):
            short = dot_nt(left[start : start + rows], right)
            residual = (weight_both * short).astype(bf16)
            hidden = jnp.dot(residual, back, preferred_element_type=f32)
            part = resp[start : start + rows]
            same = same + part * hidden
            cross = cross + part * swap(hidden)
        real = same + swap(same)
        imag = swap(cross) - cross
        energy = jnp.where(lanes(real.shape) < half, real, imag)
        height = everyone // len(SENT)
        for low_row in range(0, rows, height):
            place = SENT[(start + low_row) // height] * height
            out_ref[place : place + height] = energy[low_row : low_row + height]


def slabs(data_ref, first, count):
    everyone = data_ref.shape[0] * data_ref.shape[2]
    return [
        data_ref[:, first + i].astype(f32).reshape(everyone, data_ref.shape[3])
        for i in range(count)
    ]


def first_body(bands, rows, data_ref, both_ref, gain_ref, out_ref, weight_ref):
    weight_ref[...] = weigh(slabs(data_ref, 2 * bands, 1)[0], both_ref[...])
    energy_of(
        slabs(data_ref, 0, bands),
        slabs(data_ref, bands, bands),
        gain_ref[...],
        weight_ref,
        out_ref,
        rows,
    )


def next_body(bands, rows, total_ref, step_ref, gain_ref, data_ref, weight_ref, out_ref, scale_ref):
    everyone, width = gain_ref.shape
    gradient = total_ref[...].reshape(everyone, width) * (-4.0 / width)
    square = jnp.sum(jnp.sum(gradient * gradient, axis=0, keepdims=True), axis=1, keepdims=True)
    scale = 1.0 / jnp.sqrt(square * (2.0 / (everyone * width)) + 1e-06)
    scale_ref[...] = jnp.broadcast_to(scale, scale_ref.shape)
    gains = gain_ref[...] - step_ref[...] * (gradient * scale)
    energy_of(slabs(data_ref, 0, bands), slabs(data_ref, bands, bands), gains, weight_ref, out_ref, rows)


def sum_body(in_ref, out_ref, grad_ref):
    total = jnp.sum(in_ref[...], axis=0)
    out_ref[...] = jnp.broadcast_to(total[None], out_ref.shape)
    grad_ref[...] = total * (-4.0 / in_ref.shape[2])


def split_out_body(in_ref, out_ref):
    blocks, stations = 2, out_ref.shape[1]
    total = jnp.sum(in_ref[...], axis=0)
    each = out_ref.shape[0] // blocks
    for block in range(blocks):
        piece = total[block * stations : (block + 1) * stations]
        out_ref[block * each : (block + 1) * each] = jnp.broadcast_to(piece[None], (each,) + piece.shape)


def square_body(in_ref, grad_ref, out_ref):
    width = in_ref.shape[2]
    gradient = jnp.sum(in_ref[...], axis=0) * (-4.0 / width)
    grad_ref[...] = gradient
    square = jnp.sum(gradient * gradient, axis=0, keepdims=True)
    out_ref[...] = jnp.broadcast_to(square[None], out_ref.shape)


def last_body(everyone, square_ref, grad_ref, gain_ref, step_ref, before_ref, scale_ref, out_ref, descent_ref):
    width = grad_ref.shape[1]
    square = jnp.sum(jnp.sum(square_ref[...], axis=0), axis=1, keepdims=True)
    descent = grad_ref[...] * (1.0 / jnp.sqrt(square * (2.0 / (everyone * width)) + 1e-06))
    gains = gain_ref[...] - step_ref[...] * (before_ref[...] * scale_ref[...])
    descent_ref[...] = descent
    out_ref[...] = gains - step_ref[...] * descent


def shards(voltages, response, start_gains, step_sizes, station_ids, baseline_flags):
    stations, bands, times, width = voltages.shape
    plane = lax.axis_size(PLANE)
    ring = lax.axis_size(ROUND)
    column = lax.axis_size(COLUMN)
    everyone = stations * ring
    rows = 256
    shape = jax.ShapeDtypeStruct
    step = step_sizes[None, :]
    at = lax.axis_index(STN).reshape(1)

    def swap_over(values, axis):
        return lax.all_to_all(values, axis, split_axis=0, concat_axis=0, tiled=True)

    packed = call(
        pack_body,
        shape((ring, 2 * bands + 1, stations, width), bf16),
        tuple(
            pltpu.with_memory_space_constraint(a, pltpu.HBM)
            for a in (station_ids, voltages, response)
        ),
        "pack",
        left=(0, 1, 2),
        scratch=(
            pltpu.SMEM((stations,), jnp.int32),
            pltpu.VMEM((2 * bands, stations, times, width), bf16),
            pltpu.SemaphoreType.DMA((2 * bands + 1,)),
        ),
    )
    data = swap_over(packed, ROUND)
    both, own, wide, held = call(
        functools.partial(ready_body, stations),
        (
            shape((everyone, everyone), bf16),
            shape((stations, width), f32),
            shape((1, width), f32),
            shape((everyone, width), f32),
        ),
        (at, baseline_flags, start_gains, step),
        "ready",
        smem=(0,),
    )
    energy, weight = call(
        functools.partial(first_body, bands, rows),
        (shape((everyone, width), f32), shape((everyone, everyone), f32)),
        (data, both, held),
        "first",
    )

    def reduced(energy):
        parts = swap_over(energy.reshape(plane, everyone // plane, width), PLANE)
        copies = call(split_out_body, shape((column, stations, width), f32), (parts,), "split")
        return swap_over(copies, COLUMN)

    copies, before = call(
        sum_body,
        (shape((ring, stations, width), f32), shape((stations, width), f32)),
        (reduced(energy),),
        "sum",
    )
    total = swap_over(copies, ROUND)
    energy, scale = call(
        functools.partial(next_body, bands, rows),
        (shape((everyone, width), f32), shape((1, width), f32)),
        (total, wide, held, data, weight),
        "next",
    )
    gradient, square = call(
        square_body,
        (shape((stations, width), f32), shape((ring, 1, width), f32)),
        (reduced(energy),),
        "square",
    )
    squares = swap_over(square, ROUND)
    return call(
        functools.partial(last_body, everyone),
        (shape((stations, width), f32), shape((stations, width), f32)),
        (squares, gradient, own, wide, before, scale),
        "last",
    )


def solution(mesh):
    devices = mesh.devices
    finer = Mesh(devices.reshape((2,) * len(STN) + devices.shape[1:]), STN + ("chan",))
    placed = (P(STN, "chan", None, None), P(STN, "chan", None, None), P(), P(), P(STN), P())
    return jax.shard_map(
        shards,
        mesh=finer,
        in_specs=placed,
        out_specs=(P(STN, None), P(STN, None)),
        check_vma=False,
    )
```

```python
import functools

import jax
import jax.numpy as jnp
import numpy as np
from jax import lax
from jax.experimental import pallas as pl
from jax.experimental.pallas import tpu as pltpu
from jax.sharding import Mesh
from jax.sharding import PartitionSpec as P

LIMIT = 48 * 1024 * 1024
STN = ("x1", "x0", "y2", "y1", "y0", "pair")
ROUND = ("y2", "x1", "y1", "pair", "y0", "x0")
PLANE = ("y2", "x1", "y1", "y0", "x0")
COLUMN = ("pair", "chan")


def numbered(axes):
    whole = np.arange(2 ** len(STN)).reshape((2,) * len(STN))
    return whole.transpose([STN.index(axis) for axis in axes]).reshape(-1)


HELD = [int(number) for number in numbered(ROUND)]
SENT = [int(place) for place in np.argsort(numbered(PLANE + ("pair",)))[numbered(ROUND)]]
f32 = jnp.float32
bf16 = jnp.bfloat16


def call(body, outs, args, name, smem=(), left=(), scratch=()):
    specs = [
        pl.BlockSpec(memory_space=pltpu.SMEM if i in smem else pltpu.HBM if i in left else pltpu.VMEM)
        for i in range(len(args))
    ]
    single = not isinstance(outs, (tuple, list))
    listed = [outs] if single else list(outs)
    result = pl.pallas_call(
        body,
        out_shape=listed,
        in_specs=specs,
        out_specs=[pl.BlockSpec(memory_space=pltpu.VMEM) for _ in listed],
        scratch_shapes=list(scratch),
        compiler_params=pltpu.CompilerParams(vmem_limit_bytes=LIMIT),
        name=name,
    )(*args)
    return result[0] if single else result


def lanes(shape):
    return lax.broadcasted_iota(jnp.int32, shape, len(shape) - 1)


def swap(values):
    half = values.shape[-1] // 2
    return pltpu.roll(values, half, values.ndim - 1)


def rotate(values):
    half = values.shape[-1] // 2
    turned = swap(values)
    return jnp.where(lanes(values.shape) < half, -turned, turned)


def pack_body(
    at_ref, ids_from, volt_from, resp_from, flag_from, gain_from, step_from,
    out_ref, both_ref, own_ref, wide_ref, mixed_ref,
    ids_ref, held, flag_ref, gain_ref, step_ref, sems,
):
    bands, stations = held.shape[0] // 2, held.shape[1]
    copies = [
        pltpu.make_async_copy(ref.at[:, band], held.at[slot + band], sems.at[slot + band])
        for slot, ref in ((0, volt_from), (bands, resp_from))
        for band in range(bands)
    ]
    more = [
        pltpu.make_async_copy(source, target, sems.at[2 * bands + i])
        for i, (source, target) in enumerate(
            (
                (ids_from, ids_ref),
                (step_from, step_ref),
                (gain_from, gain_ref),
                (flag_from, flag_ref),
            )
        )
    ]
    for copy in copies + more:
        copy.start()
    more[0].wait()
    row = lax.broadcasted_iota(jnp.int32, out_ref.shape[2:], 0)
    number = jnp.zeros(row.shape, f32)
    for station in range(stations):
        number = jnp.where(row == station, (ids_ref[station] - 256).astype(f32), number)
    out_ref[:, 2 * bands] = jnp.broadcast_to(number[None], (out_ref.shape[0],) + row.shape).astype(bf16)
    for slot, copy in enumerate(copies):
        copy.wait()
        out_ref[:, slot] = jnp.transpose(held[slot].astype(f32), (1, 0, 2)).astype(bf16)
    more[1].wait()
    wide_ref[...] = jnp.concatenate([step_ref[...], step_ref[...]], axis=1)
    more[2].wait()
    own_ref[...] = gain_ref[pl.ds(pl.multiple_of(at_ref[0] * stations, stations), stations)]
    for place, source in enumerate(HELD):
        mixed_ref[place * stations : (place + 1) * stations] = gain_ref[
            source * stations : (source + 1) * stations
        ]
    more[3].wait()
    flags = flag_ref[...].astype(f32)
    both_ref[...] = (flags * flags.T).astype(bf16)


def dot_nt(left, right):
    return lax.dot_general(left, right, (((1,), (1,)), ((), ())), preferred_element_type=f32)


def weigh(number, both):
    everyone, width = number.shape
    pieces = [
        number == (lanes(number.shape) + (piece * width - 256)).astype(f32)
        for piece in range(everyone // width)
    ]
    chosen = jnp.concatenate([jnp.where(p, 1.0, 0.0).astype(bf16) for p in pieces], axis=1)
    half = jnp.dot(chosen, both, preferred_element_type=f32).astype(bf16)
    picked = dot_nt(half, chosen)
    rows = lax.broadcasted_iota(jnp.int32, picked.shape, 0)
    return jnp.where(rows == lanes(picked.shape), 0.0, picked * (1.0 / 64.0))


def energy_of(volts, resps, gains, weight_ref, out_ref, rows):
    everyone, width = gains.shape
    half = width // 2
    low = lanes(gains.shape) < half
    turned = swap(gains)
    straight = jnp.where(low, gains, turned)
    crossed = jnp.where(low, -turned, gains)
    lefts, rights, backs = [], [], []
    for volt, resp in zip(volts, resps):
        applied = (straight * resp + crossed * swap(resp)).astype(bf16)
        applied_float = applied.astype(f32)
        turned_applied = rotate(applied_float).astype(bf16)
        volt_low = volt.astype(bf16)
        lefts.append(jnp.concatenate([volt_low, (-applied_float).astype(bf16)], axis=1))
        rights.append(
            jnp.concatenate(
                [
                    jnp.concatenate([volt_low, applied], axis=1),
                    jnp.concatenate([rotate(volt).astype(bf16), turned_applied], axis=1),
                ],
                axis=0,
            )
        )
        backs.append(jnp.concatenate([applied, turned_applied], axis=0))
    for start in range(0, everyone, rows):
        weight = weight_ref[start : start + rows]
        weight_both = jnp.concatenate([weight, weight], axis=1)
        same = cross = 0.0
        for left, right, back, resp in zip(lefts, rights, backs, resps):
            short = dot_nt(left[start : start + rows], right)
            residual = (weight_both * short).astype(bf16)
            hidden = jnp.dot(residual, back, preferred_element_type=f32)
            part = resp[start : start + rows]
            same = same + part * hidden
            cross = cross + part * swap(hidden)
        real = same + swap(same)
        imag = swap(cross) - cross
        energy = jnp.where(lanes(real.shape) < half, real, imag)
        height = everyone // len(SENT)
        for low_row in range(0, rows, height):
            place = SENT[(start + low_row) // height] * height
            out_ref[place : place + height] = energy[low_row : low_row + height]


def slabs(data_ref, first, count):
    everyone = data_ref.shape[0] * data_ref.shape[2]
    return [
        data_ref[:, first + i].astype(f32).reshape(everyone, data_ref.shape[3])
        for i in range(count)
    ]


def first_body(bands, rows, data_ref, both_ref, gain_ref, out_ref, weight_ref):
    weight_ref[...] = weigh(slabs(data_ref, 2 * bands, 1)[0], both_ref[...])
    energy_of(
        slabs(data_ref, 0, bands),
        slabs(data_ref, bands, bands),
        gain_ref[...],
        weight_ref,
        out_ref,
        rows,
    )


def next_body(bands, rows, total_ref, step_ref, gain_ref, data_ref, weight_ref, out_ref, scale_ref):
    everyone, width = gain_ref.shape
    gradient = total_ref[...].reshape(everyone, width) * (-4.0 / width)
    square = jnp.sum(jnp.sum(gradient * gradient, axis=0, keepdims=True), axis=1, keepdims=True)
    scale = 1.0 / jnp.sqrt(square * (2.0 / (everyone * width)) + 1e-06)
    scale_ref[...] = jnp.broadcast_to(scale, scale_ref.shape)
    gains = gain_ref[...] - step_ref[...] * (gradient * scale)
    energy_of(slabs(data_ref, 0, bands), slabs(data_ref, bands, bands), gains, weight_ref, out_ref, rows)


def sum_body(in_ref, out_ref, grad_ref):
    total = jnp.sum(in_ref[...], axis=0)
    out_ref[...] = jnp.broadcast_to(total[None], out_ref.shape)
    grad_ref[...] = total * (-4.0 / in_ref.shape[2])


def split_out_body(in_ref, out_ref):
    blocks, stations = 2, out_ref.shape[1]
    total = jnp.sum(in_ref[...], axis=0)
    each = out_ref.shape[0] // blocks
    for block in range(blocks):
        piece = total[block * stations : (block + 1) * stations]
        out_ref[block * each : (block + 1) * each] = jnp.broadcast_to(piece[None], (each,) + piece.shape)


def square_body(in_ref, grad_ref, out_ref):
    width = in_ref.shape[2]
    gradient = jnp.sum(in_ref[...], axis=0) * (-4.0 / width)
    grad_ref[...] = gradient
    square = jnp.sum(gradient * gradient, axis=0, keepdims=True)
    out_ref[...] = jnp.broadcast_to(square[None], out_ref.shape)


def last_body(everyone, square_ref, grad_ref, gain_ref, step_ref, before_ref, scale_ref, out_ref, descent_ref):
    width = grad_ref.shape[1]
    square = jnp.sum(jnp.sum(square_ref[...], axis=0), axis=1, keepdims=True)
    descent = grad_ref[...] * (1.0 / jnp.sqrt(square * (2.0 / (everyone * width)) + 1e-06))
    gains = gain_ref[...] - step_ref[...] * (before_ref[...] * scale_ref[...])
    descent_ref[...] = descent
    out_ref[...] = gains - step_ref[...] * descent


def shards(voltages, response, start_gains, step_sizes, station_ids, baseline_flags):
    stations, bands, times, width = voltages.shape
    plane = lax.axis_size(PLANE)
    ring = lax.axis_size(ROUND)
    column = lax.axis_size(COLUMN)
    everyone = stations * ring
    rows = 256
    shape = jax.ShapeDtypeStruct
    step = step_sizes[None, :]
    at = lax.axis_index(STN).reshape(1)

    def swap_over(values, axis):
        return lax.all_to_all(values, axis, split_axis=0, concat_axis=0, tiled=True)

    sources = (station_ids, voltages, response, baseline_flags, start_gains, step)
    packed, both, own, wide, held = call(
        pack_body,
        (
            shape((ring, 2 * bands + 1, stations, width), bf16),
            shape((everyone, everyone), bf16),
            shape((stations, width), f32),
            shape((1, width), f32),
            shape((everyone, width), f32),
        ),
        (at,) + tuple(pltpu.with_memory_space_constraint(a, pltpu.HBM) for a in sources),
        "pack",
        smem=(0,),
        left=tuple(range(1, 7)),
        scratch=(
            pltpu.SMEM((stations,), jnp.int32),
            pltpu.VMEM((2 * bands, stations, times, width), bf16),
            pltpu.VMEM((everyone, everyone), jnp.int32),
            pltpu.VMEM((everyone, width), f32),
            pltpu.VMEM(step.shape, f32),
            pltpu.SemaphoreType.DMA((2 * bands + 4,)),
        ),
    )
    data = swap_over(packed, ROUND)
    energy, weight = call(
        functools.partial(first_body, bands, rows),
        (shape((everyone, width), f32), shape((everyone, everyone), f32)),
        (data, both, held),
        "first",
    )

    def reduced(energy):
        parts = swap_over(energy.reshape(plane, everyone // plane, width), PLANE)
        copies = call(split_out_body, shape((column, stations, width), f32), (parts,), "split")
        return swap_over(copies, COLUMN)

    copies, before = call(
        sum_body,
        (shape((ring, stations, width), f32), shape((stations, width), f32)),
        (reduced(energy),),
        "sum",
    )
    total = swap_over(copies, ROUND)
    energy, scale = call(
        functools.partial(next_body, bands, rows),
        (shape((everyone, width), f32), shape((1, width), f32)),
        (total, wide, held, data, weight),
        "next",
    )
    gradient, square = call(
        square_body,
        (shape((stations, width), f32), shape((ring, 1, width), f32)),
        (reduced(energy),),
        "square",
    )
    squares = swap_over(square, ROUND)
    return call(
        functools.partial(last_body, everyone),
        (shape((stations, width), f32), shape((stations, width), f32)),
        (squares, gradient, own, wide, before, scale),
        "last",
    )


def solution(mesh):
    devices = mesh.devices
    finer = Mesh(devices.reshape((2,) * len(STN) + devices.shape[1:]), STN + ("chan",))
    placed = (P(STN, "chan", None, None), P(STN, "chan", None, None), P(), P(), P(STN), P())
    return jax.shard_map(
        shards,
        mesh=finer,
        in_specs=placed,
        out_specs=(P(STN, None), P(STN, None)),
        check_vma=False,
    )
```

```python
import functools

import jax
import jax.numpy as jnp
import numpy as np
from jax import lax
from jax.experimental import pallas as pl
from jax.experimental.pallas import tpu as pltpu
from jax.sharding import Mesh
from jax.sharding import PartitionSpec as P

LIMIT = 48 * 1024 * 1024
STN = ("x1", "x0", "y2", "y1", "y0", "pair")
ROUND = ("x1", "x0", "y2", "y1", "y0", "pair")
PLANE = ("x1", "x0", "y2", "y1", "y0")
COLUMN = ("pair", "chan")


def numbered(axes):
    whole = np.arange(2 ** len(STN)).reshape((2,) * len(STN))
    return whole.transpose([STN.index(axis) for axis in axes]).reshape(-1)


HELD = [int(number) for number in numbered(ROUND)]
SENT = [int(place) for place in np.argsort(numbered(PLANE + ("pair",)))[numbered(ROUND)]]
f32 = jnp.float32
bf16 = jnp.bfloat16


def call(body, outs, args, name, smem=(), left=(), scratch=()):
    specs = [
        pl.BlockSpec(memory_space=pltpu.SMEM if i in smem else pltpu.HBM if i in left else pltpu.VMEM)
        for i in range(len(args))
    ]
    single = not isinstance(outs, (tuple, list))
    listed = [outs] if single else list(outs)
    result = pl.pallas_call(
        body,
        out_shape=listed,
        in_specs=specs,
        out_specs=[pl.BlockSpec(memory_space=pltpu.VMEM) for _ in listed],
        scratch_shapes=list(scratch),
        compiler_params=pltpu.CompilerParams(vmem_limit_bytes=LIMIT),
        name=name,
    )(*args)
    return result[0] if single else result


def lanes(shape):
    return lax.broadcasted_iota(jnp.int32, shape, len(shape) - 1)


def swap(values):
    half = values.shape[-1] // 2
    return pltpu.roll(values, half, values.ndim - 1)


def rotate(values):
    half = values.shape[-1] // 2
    turned = swap(values)
    return jnp.where(lanes(values.shape) < half, -turned, turned)


def pack_body(
    at_ref, ids_from, volt_from, resp_from, flag_from, gain_from, step_from,
    out_ref, both_ref, own_ref, wide_ref, mixed_ref,
    ids_ref, held, flag_ref, gain_ref, step_ref, sems,
):
    bands, stations = held.shape[0] // 2, held.shape[1]
    copies = [
        pltpu.make_async_copy(ref.at[:, band], held.at[slot + band], sems.at[slot + band])
        for slot, ref in ((0, volt_from), (bands, resp_from))
        for band in range(bands)
    ]
    more = [
        pltpu.make_async_copy(source, target, sems.at[2 * bands + i])
        for i, (source, target) in enumerate(
            (
                (ids_from, ids_ref),
                (step_from, step_ref),
                (gain_from, gain_ref),
                (flag_from, flag_ref),
            )
        )
    ]
    for copy in copies + more:
        copy.start()
    more[0].wait()
    half = stations // 2
    row = lax.broadcasted_iota(jnp.int32, out_ref.shape[2:], 0)
    late = lanes(row.shape) >= row.shape[1] // 2
    number = jnp.zeros(row.shape, f32)
    for station in range(stations):
        here = (row == station % half) & (late == (station >= half))
        number = jnp.where(here, (ids_ref[station] - 256).astype(f32), number)
    out_ref[:, 4 * bands] = jnp.broadcast_to(number[None], (out_ref.shape[0],) + row.shape).astype(bf16)
    for slot, copy in enumerate(copies):
        copy.wait()
        piece = jnp.transpose(held[slot].astype(f32), (1, 0, 2))
        for part in range(2):
            out_ref[:, 2 * slot + part] = piece[:, part * half : (part + 1) * half].astype(bf16)
    more[1].wait()
    wide_ref[...] = jnp.concatenate([step_ref[...], step_ref[...]], axis=1)
    more[2].wait()
    own_ref[...] = gain_ref[pl.ds(pl.multiple_of(at_ref[0] * stations, stations), stations)]
    for place, source in enumerate(HELD):
        mixed_ref[place * stations : (place + 1) * stations] = gain_ref[
            source * stations : (source + 1) * stations
        ]
    more[3].wait()
    flags = flag_ref[...].astype(f32)
    both_ref[...] = (flags * flags.T).astype(bf16)


def dot_nt(left, right):
    return lax.dot_general(left, right, (((1,), (1,)), ((), ())), preferred_element_type=f32)


def weigh(number, both):
    everyone, width = number.shape
    pieces = [
        number == (lanes(number.shape) + (piece * width - 256)).astype(f32)
        for piece in range(everyone // width)
    ]
    chosen = jnp.concatenate([jnp.where(p, 1.0, 0.0).astype(bf16) for p in pieces], axis=1)
    half = jnp.dot(chosen, both, preferred_element_type=f32).astype(bf16)
    picked = dot_nt(half, chosen)
    rows = lax.broadcasted_iota(jnp.int32, picked.shape, 0)
    return jnp.where(rows == lanes(picked.shape), 0.0, picked * (1.0 / 64.0))


def energy_of(volts, resps, gains, weight_ref, out_ref, rows):
    everyone, width = gains.shape
    half = width // 2
    low = lanes(gains.shape) < half
    turned = swap(gains)
    straight = jnp.where(low, gains, turned)
    crossed = jnp.where(low, -turned, gains)
    lefts, rights, backs = [], [], []
    for volt, resp in zip(volts, resps):
        applied = (straight * resp + crossed * swap(resp)).astype(bf16)
        applied_float = applied.astype(f32)
        turned_applied = rotate(applied_float).astype(bf16)
        volt_low = volt.astype(bf16)
        lefts.append(jnp.concatenate([volt_low, (-applied_float).astype(bf16)], axis=1))
        rights.append(
            jnp.concatenate(
                [
                    jnp.concatenate([volt_low, applied], axis=1),
                    jnp.concatenate([rotate(volt).astype(bf16), turned_applied], axis=1),
                ],
                axis=0,
            )
        )
        backs.append(jnp.concatenate([applied, turned_applied], axis=0))
    for start in range(0, everyone, rows):
        weight = weight_ref[start : start + rows]
        weight_both = jnp.concatenate([weight, weight], axis=1)
        same = cross = 0.0
        for left, right, back, resp in zip(lefts, rights, backs, resps):
            short = dot_nt(left[start : start + rows], right)
            residual = (weight_both * short).astype(bf16)
            hidden = jnp.dot(residual, back, preferred_element_type=f32)
            part = resp[start : start + rows]
            same = same + part * hidden
            cross = cross + part * swap(hidden)
        real = same + swap(same)
        imag = swap(cross) - cross
        energy = jnp.where(lanes(real.shape) < half, real, imag)
        height = everyone // len(SENT)
        for low_row in range(0, rows, height):
            place = SENT[(start + low_row) // height] * height
            out_ref[place : place + height] = energy[low_row : low_row + height]


def slabs(data_ref, first, count):
    devices, _, half, width = data_ref.shape
    found = []
    for slot in range(first, first + count):
        parts = [data_ref[:, 2 * slot + part].astype(f32) for part in range(2)]
        found.append(jnp.concatenate(parts, axis=1).reshape(devices * 2 * half, width))
    return found


def numbers(data_ref):
    devices, slots, half, width = data_ref.shape
    both = data_ref[:, slots - 1].astype(f32)
    turned = swap(both)
    low = lanes(both.shape) < width // 2
    parts = [jnp.where(low, both, turned), jnp.where(low, turned, both)]
    return jnp.concatenate(parts, axis=1).reshape(devices * 2 * half, width)


def first_body(bands, rows, data_ref, both_ref, gain_ref, out_ref, weight_ref):
    weight_ref[...] = weigh(numbers(data_ref), both_ref[...])
    energy_of(
        slabs(data_ref, 0, bands),
        slabs(data_ref, bands, bands),
        gain_ref[...],
        weight_ref,
        out_ref,
        rows,
    )


def next_body(bands, rows, total_ref, step_ref, gain_ref, data_ref, weight_ref, out_ref, scale_ref):
    everyone, width = gain_ref.shape
    gradient = total_ref[...].reshape(everyone, width) * (-4.0 / width)
    square = jnp.sum(jnp.sum(gradient * gradient, axis=0, keepdims=True), axis=1, keepdims=True)
    scale = 1.0 / jnp.sqrt(square * (2.0 / (everyone * width)) + 1e-06)
    scale_ref[...] = jnp.broadcast_to(scale, scale_ref.shape)
    gains = gain_ref[...] - step_ref[...] * (gradient * scale)
    energy_of(slabs(data_ref, 0, bands), slabs(data_ref, bands, bands), gains, weight_ref, out_ref, rows)


def sum_body(in_ref, out_ref, grad_ref):
    total = jnp.sum(in_ref[...], axis=0)
    out_ref[...] = jnp.broadcast_to(total[None], out_ref.shape)
    grad_ref[...] = total * (-4.0 / in_ref.shape[2])


def split_out_body(in_ref, out_ref):
    blocks, stations = 2, out_ref.shape[1]
    total = jnp.sum(in_ref[...], axis=0)
    each = out_ref.shape[0] // blocks
    for block in range(blocks):
        piece = total[block * stations : (block + 1) * stations]
        out_ref[block * each : (block + 1) * each] = jnp.broadcast_to(piece[None], (each,) + piece.shape)


def square_body(in_ref, grad_ref, out_ref):
    width = in_ref.shape[2]
    gradient = jnp.sum(in_ref[...], axis=0) * (-4.0 / width)
    grad_ref[...] = gradient
    square = jnp.sum(gradient * gradient, axis=0, keepdims=True)
    out_ref[...] = jnp.broadcast_to(square[None], out_ref.shape)


def last_body(everyone, square_ref, grad_ref, gain_ref, step_ref, before_ref, scale_ref, out_ref, descent_ref):
    width = grad_ref.shape[1]
    square = jnp.sum(jnp.sum(square_ref[...], axis=0), axis=1, keepdims=True)
    descent = grad_ref[...] * (1.0 / jnp.sqrt(square * (2.0 / (everyone * width)) + 1e-06))
    gains = gain_ref[...] - step_ref[...] * (before_ref[...] * scale_ref[...])
    descent_ref[...] = descent
    out_ref[...] = gains - step_ref[...] * descent


def shards(voltages, response, start_gains, step_sizes, station_ids, baseline_flags):
    stations, bands, times, width = voltages.shape
    plane = lax.axis_size(PLANE)
    ring = lax.axis_size(ROUND)
    column = lax.axis_size(COLUMN)
    everyone = stations * ring
    rows = 256
    shape = jax.ShapeDtypeStruct
    step = step_sizes[None, :]
    at = lax.axis_index(STN).reshape(1)

    def swap_over(values, axis):
        return lax.all_to_all(values, axis, split_axis=0, concat_axis=0, tiled=True)

    sources = (station_ids, voltages, response, baseline_flags, start_gains, step)
    packed, both, own, wide, held = call(
        pack_body,
        (
            shape((ring, 4 * bands + 1, stations // 2, width), bf16),
            shape((everyone, everyone), bf16),
            shape((stations, width), f32),
            shape((1, width), f32),
            shape((everyone, width), f32),
        ),
        (at,) + tuple(pltpu.with_memory_space_constraint(a, pltpu.HBM) for a in sources),
        "pack",
        smem=(0,),
        left=tuple(range(1, 7)),
        scratch=(
            pltpu.SMEM((stations,), jnp.int32),
            pltpu.VMEM((2 * bands, stations, times, width), bf16),
            pltpu.VMEM((everyone, everyone), jnp.int32),
            pltpu.VMEM((everyone, width), f32),
            pltpu.VMEM(step.shape, f32),
            pltpu.SemaphoreType.DMA((2 * bands + 4,)),
        ),
    )
    data = swap_over(packed, ROUND)
    energy, weight = call(
        functools.partial(first_body, bands, rows),
        (shape((everyone, width), f32), shape((everyone, everyone), f32)),
        (data, both, held),
        "first",
    )

    def reduced(energy):
        parts = swap_over(energy.reshape(plane, everyone // plane, width), PLANE)
        copies = call(split_out_body, shape((column, stations, width), f32), (parts,), "split")
        return swap_over(copies, COLUMN)

    copies, before = call(
        sum_body,
        (shape((ring, stations, width), f32), shape((stations, width), f32)),
        (reduced(energy),),
        "sum",
    )
    total = swap_over(copies, ROUND)
    energy, scale = call(
        functools.partial(next_body, bands, rows),
        (shape((everyone, width), f32), shape((1, width), f32)),
        (total, wide, held, data, weight),
        "next",
    )
    gradient, square = call(
        square_body,
        (shape((stations, width), f32), shape((ring, 1, width), f32)),
        (reduced(energy),),
        "square",
    )
    squares = swap_over(square, ROUND)
    return call(
        functools.partial(last_body, everyone),
        (shape((stations, width), f32), shape((stations, width), f32)),
        (squares, gradient, own, wide, before, scale),
        "last",
    )


def solution(mesh):
    devices = mesh.devices
    finer = Mesh(devices.reshape((2,) * len(STN) + devices.shape[1:]), STN + ("chan",))
    placed = (P(STN, "chan", None, None), P(STN, "chan", None, None), P(), P(), P(STN), P())
    return jax.shard_map(
        shards,
        mesh=finer,
        in_specs=placed,
        out_specs=(P(STN, None), P(STN, None)),
        check_vma=False,
    )
```

```python
import functools

import jax
import jax.numpy as jnp
from jax import lax
from jax.experimental import pallas as pl
from jax.experimental.pallas import tpu as pltpu
from jax.sharding import Mesh
from jax.sharding import PartitionSpec as P

LIMIT = 48 * 1024 * 1024
f32 = jnp.float32
bf16 = jnp.bfloat16
exact = jnp.float8_e4m3fn


def call(body, outs, args, name, smem=(), left=(), scratch=()):
    specs = [
        pl.BlockSpec(memory_space=pltpu.SMEM if i in smem else pltpu.HBM if i in left else pltpu.VMEM)
        for i in range(len(args))
    ]
    single = not isinstance(outs, (tuple, list))
    listed = [outs] if single else list(outs)
    result = pl.pallas_call(
        body,
        out_shape=listed,
        in_specs=specs,
        out_specs=[pl.BlockSpec(memory_space=pltpu.VMEM) for _ in listed],
        scratch_shapes=list(scratch),
        compiler_params=pltpu.CompilerParams(vmem_limit_bytes=LIMIT),
        name=name,
    )(*args)
    return result[0] if single else result


def lanes(shape):
    return lax.broadcasted_iota(jnp.int32, shape, len(shape) - 1)


def swap(values):
    half = values.shape[-1] // 2
    return pltpu.roll(values, half, values.ndim - 1)


def rotate(values):
    half = values.shape[-1] // 2
    turned = swap(values)
    return jnp.where(lanes(values.shape) < half, -turned, turned)


def pack_body(
    at_ref, ids_from, volt_from, resp_from, gain_from, step_from,
    out_ref, own_ref, wide_ref, gain_ref,
    ids_ref, held, step_ref, sems,
):
    bands, stations = held.shape[0] // 2, held.shape[1]
    copies = [
        pltpu.make_async_copy(ref.at[:, band], held.at[slot + band], sems.at[slot + band])
        for slot, ref in ((0, volt_from), (bands, resp_from))
        for band in range(bands)
    ]
    more = [
        pltpu.make_async_copy(source, target, sems.at[2 * bands + i])
        for i, (source, target) in enumerate(
            ((ids_from, ids_ref), (step_from, step_ref), (gain_from, gain_ref))
        )
    ]
    for copy in copies + more:
        copy.start()
    more[0].wait()
    half = stations // 2
    row = lax.broadcasted_iota(jnp.int32, out_ref.shape[2:], 0)
    late = lanes(row.shape) >= row.shape[1] // 2
    number = jnp.zeros(row.shape, f32)
    for station in range(stations):
        here = (row == station % half) & (late == (station >= half))
        number = jnp.where(here, (ids_ref[station] - 256).astype(f32), number)
    out_ref[:, 4 * bands] = jnp.broadcast_to(number[None], (out_ref.shape[0],) + row.shape).astype(bf16)
    for slot, copy in enumerate(copies):
        copy.wait()
        piece = jnp.transpose(held[slot].astype(f32), (1, 0, 2))
        for part in range(2):
            out_ref[:, 2 * slot + part] = piece[:, part * half : (part + 1) * half].astype(bf16)
    more[1].wait()
    wide_ref[...] = jnp.concatenate([step_ref[...], step_ref[...]], axis=1)
    more[2].wait()
    own_ref[...] = gain_ref[pl.ds(pl.multiple_of(at_ref[0] * stations, stations), stations)]


def dot_nt(left, right):
    return lax.dot_general(left, right, (((1,), (1,)), ((), ())), preferred_element_type=f32)


def weigh(number, both):
    everyone, width = number.shape
    pieces = [
        number == (lanes(number.shape) + (piece * width - 256)).astype(f32)
        for piece in range(everyone // width)
    ]
    chosen = jnp.concatenate([jnp.where(p, 1.0, 0.0).astype(exact) for p in pieces], axis=1)
    half = jnp.dot(chosen, both, preferred_element_type=f32).astype(exact)
    picked = dot_nt(half, chosen)
    rows = lax.broadcasted_iota(jnp.int32, picked.shape, 0)
    return jnp.where(rows == lanes(picked.shape), 0.0, picked * (1.0 / 64.0)).astype(bf16)


def energy_of(volts, resps, gains, weight_ref, out_ref, rows):
    everyone, width = gains.shape
    half = width // 2
    low = lanes(gains.shape) < half
    turned = swap(gains)
    straight = jnp.where(low, gains, turned)
    crossed = jnp.where(low, -turned, gains)
    lefts, rights, backs = [], [], []
    for volt, resp in zip(volts, resps):
        applied = (straight * resp + crossed * swap(resp)).astype(bf16)
        applied_float = applied.astype(f32)
        turned_applied = rotate(applied_float).astype(bf16)
        volt_low = volt.astype(bf16)
        lefts.append(jnp.concatenate([volt_low, (-applied_float).astype(bf16)], axis=1))
        rights.append(
            jnp.concatenate(
                [
                    jnp.concatenate([volt_low, applied], axis=1),
                    jnp.concatenate([rotate(volt).astype(bf16), turned_applied], axis=1),
                ],
                axis=0,
            )
        )
        backs.append(jnp.concatenate([applied, turned_applied], axis=0))
    for start in range(0, everyone, rows):
        weight = weight_ref[start : start + rows]
        weight_both = jnp.concatenate([weight, weight], axis=1)
        same = cross = 0.0
        for left, right, back, resp in zip(lefts, rights, backs, resps):
            short = dot_nt(left[start : start + rows], right)
            residual = weight_both * short.astype(bf16)
            hidden = jnp.dot(residual, back, preferred_element_type=f32)
            part = resp[start : start + rows]
            same = same + part * hidden
            cross = cross + part * swap(hidden)
        real = same + swap(same)
        imag = swap(cross) - cross
        out_ref[start : start + rows] = jnp.where(lanes(real.shape) < half, real, imag)


def slabs(data_ref, first, count):
    devices, _, half, width = data_ref.shape
    found = []
    for slot in range(first, first + count):
        parts = [data_ref[:, 2 * slot + part].astype(f32) for part in range(2)]
        found.append(jnp.concatenate(parts, axis=1).reshape(devices * 2 * half, width))
    return found


def numbers(data_ref):
    devices, slots, half, width = data_ref.shape
    both = data_ref[:, slots - 1].astype(f32)
    turned = swap(both)
    low = lanes(both.shape) < width // 2
    parts = [jnp.where(low, both, turned), jnp.where(low, turned, both)]
    return jnp.concatenate(parts, axis=1).reshape(devices * 2 * half, width)


def first_body(bands, rows, data_ref, flag_ref, gain_ref, out_ref, weight_ref):
    flags = flag_ref[...].astype(f32)
    weight_ref[...] = weigh(numbers(data_ref), (flags * flags.T).astype(exact))
    energy_of(
        slabs(data_ref, 0, bands),
        slabs(data_ref, bands, bands),
        gain_ref[...],
        weight_ref,
        out_ref,
        rows,
    )


def next_body(bands, rows, total_ref, step_ref, gain_ref, data_ref, weight_ref, out_ref, scale_ref):
    everyone, width = gain_ref.shape
    gradient = total_ref[...].reshape(everyone, width) * (-4.0 / width)
    square = jnp.sum(jnp.sum(gradient * gradient, axis=0, keepdims=True), axis=1, keepdims=True)
    scale = 1.0 / jnp.sqrt(square * (2.0 / (everyone * width)) + 1e-06)
    scale_ref[...] = jnp.broadcast_to(scale, scale_ref.shape)
    gains = gain_ref[...] - step_ref[...] * (gradient * scale)
    energy_of(slabs(data_ref, 0, bands), slabs(data_ref, bands, bands), gains, weight_ref, out_ref, rows)


def sum_body(in_ref, out_ref, grad_ref):
    total = jnp.sum(in_ref[...], axis=0)
    out_ref[...] = jnp.broadcast_to(total[None], out_ref.shape)
    grad_ref[...] = total * (-4.0 / in_ref.shape[2])


def split_out_body(in_ref, out_ref):
    blocks, stations = 2, out_ref.shape[1]
    total = jnp.sum(in_ref[...], axis=0)
    each = out_ref.shape[0] // blocks
    for block in range(blocks):
        piece = total[block * stations : (block + 1) * stations]
        out_ref[block * each : (block + 1) * each] = jnp.broadcast_to(piece[None], (each,) + piece.shape)


def square_body(in_ref, grad_ref, out_ref):
    width = in_ref.shape[2]
    gradient = jnp.sum(in_ref[...], axis=0) * (-4.0 / width)
    grad_ref[...] = gradient
    square = jnp.sum(gradient * gradient, axis=0, keepdims=True)
    out_ref[...] = jnp.broadcast_to(square[None], out_ref.shape)


def last_body(everyone, square_ref, grad_ref, gain_ref, step_ref, before_ref, scale_ref, out_ref, descent_ref):
    width = grad_ref.shape[1]
    square = jnp.sum(jnp.sum(square_ref[...], axis=0), axis=1, keepdims=True)
    descent = grad_ref[...] * (1.0 / jnp.sqrt(square * (2.0 / (everyone * width)) + 1e-06))
    gains = gain_ref[...] - step_ref[...] * (before_ref[...] * scale_ref[...])
    descent_ref[...] = descent
    out_ref[...] = gains - step_ref[...] * descent


def shards(voltages, response, start_gains, step_sizes, station_ids, baseline_flags):
    stations, bands, times, width = voltages.shape
    stn = ("plane", "pair")
    plane = lax.axis_size("plane")
    ring = lax.axis_size(stn)
    column = lax.axis_size(("pair", "chan"))
    everyone = stations * ring
    rows = 256
    shape = jax.ShapeDtypeStruct
    step = step_sizes[None, :]
    at = lax.axis_index(stn).reshape(1)

    def swap_over(values, axis):
        return lax.all_to_all(values, axis, split_axis=0, concat_axis=0, tiled=True)

    sources = (station_ids, voltages, response, start_gains, step)
    packed, own, wide, held = call(
        pack_body,
        (
            shape((ring, 4 * bands + 1, stations // 2, width), bf16),
            shape((stations, width), f32),
            shape((1, width), f32),
            shape((everyone, width), f32),
        ),
        (at,) + tuple(pltpu.with_memory_space_constraint(a, pltpu.HBM) for a in sources),
        "pack",
        smem=(0,),
        left=tuple(range(1, 6)),
        scratch=(
            pltpu.SMEM((stations,), jnp.int32),
            pltpu.VMEM((2 * bands, stations, times, width), bf16),
            pltpu.VMEM(step.shape, f32),
            pltpu.SemaphoreType.DMA((2 * bands + 3,)),
        ),
    )
    data = swap_over(packed, stn)
    energy, weight = call(
        functools.partial(first_body, bands, rows),
        (shape((everyone, width), f32), shape((everyone, everyone), bf16)),
        (data, baseline_flags, held),
        "first",
    )

    def reduced(energy):
        parts = swap_over(energy.reshape(plane, everyone // plane, width), "plane")
        copies = call(split_out_body, shape((column, stations, width), f32), (parts,), "split")
        return swap_over(copies, ("pair", "chan"))

    copies, before = call(
        sum_body,
        (shape((ring, stations, width), f32), shape((stations, width), f32)),
        (reduced(energy),),
        "sum",
    )
    total = swap_over(copies, stn)
    energy, scale = call(
        functools.partial(next_body, bands, rows),
        (shape((everyone, width), f32), shape((1, width), f32)),
        (total, wide, held, data, weight),
        "next",
    )
    gradient, square = call(
        square_body,
        (shape((stations, width), f32), shape((ring, 1, width), f32)),
        (reduced(energy),),
        "square",
    )
    squares = swap_over(square, stn)
    return call(
        functools.partial(last_body, everyone),
        (shape((stations, width), f32), shape((stations, width), f32)),
        (squares, gradient, own, wide, before, scale),
        "last",
    )


def solution(mesh):
    pair = 2
    devices = mesh.devices
    finer = Mesh(
        devices.reshape(devices.shape[0] // pair, pair, devices.shape[1]), ("plane", "pair", "chan")
    )
    stn = ("plane", "pair")
    placed = (P(stn, "chan", None, None), P(stn, "chan", None, None), P(), P(), P(stn), P())
    return jax.shard_map(
        shards,
        mesh=finer,
        in_specs=placed,
        out_specs=(P(stn, None), P(stn, None)),
        check_vma=False,
    )
```

```python
import functools

import jax
import jax.numpy as jnp
from jax import lax
from jax.experimental import pallas as pl
from jax.experimental.pallas import tpu as pltpu
from jax.sharding import Mesh
from jax.sharding import PartitionSpec as P

LIMIT = 48 * 1024 * 1024
f32 = jnp.float32
bf16 = jnp.bfloat16
exact = jnp.float8_e4m3fn


def call(body, outs, args, name, smem=(), left=(), scratch=()):
    specs = [
        pl.BlockSpec(memory_space=pltpu.SMEM if i in smem else pltpu.HBM if i in left else pltpu.VMEM)
        for i in range(len(args))
    ]
    single = not isinstance(outs, (tuple, list))
    listed = [outs] if single else list(outs)
    result = pl.pallas_call(
        body,
        out_shape=listed,
        in_specs=specs,
        out_specs=[pl.BlockSpec(memory_space=pltpu.VMEM) for _ in listed],
        scratch_shapes=list(scratch),
        compiler_params=pltpu.CompilerParams(vmem_limit_bytes=LIMIT),
        name=name,
    )(*args)
    return result[0] if single else result


def lanes(shape):
    return lax.broadcasted_iota(jnp.int32, shape, len(shape) - 1)


def swap(values):
    half = values.shape[-1] // 2
    return pltpu.roll(values, half, values.ndim - 1)


def rotate(values):
    half = values.shape[-1] // 2
    turned = swap(values)
    return jnp.where(lanes(values.shape) < half, -turned, turned)


def pack_body(
    at_ref, ids_from, volt_from, resp_from, gain_from, step_from,
    out_ref, own_ref, wide_ref, gain_ref,
    ids_ref, held, step_ref, sems,
):
    bands, stations = held.shape[0] // 2, held.shape[1]
    copies = [
        pltpu.make_async_copy(ref.at[:, band], held.at[slot + band], sems.at[slot + band])
        for slot, ref in ((0, volt_from), (bands, resp_from))
        for band in range(bands)
    ]
    more = [
        pltpu.make_async_copy(source, target, sems.at[2 * bands + i])
        for i, (source, target) in enumerate(
            ((ids_from, ids_ref), (step_from, step_ref), (gain_from, gain_ref))
        )
    ]
    for copy in copies + more:
        copy.start()
    more[0].wait()
    height, columns = out_ref.shape[2:]
    parts = stations // height
    row = lax.broadcasted_iota(jnp.int32, (height, columns), 0)
    column = lanes(row.shape) // (columns // parts)
    number = jnp.zeros(row.shape, f32)
    for station in range(stations):
        here = (row == station % height) & (column == station // height)
        number = jnp.where(here, (ids_ref[station] - 256).astype(f32), number)
    out_ref[:, 2 * bands * parts] = jnp.broadcast_to(
        number[None], (out_ref.shape[0],) + row.shape
    ).astype(bf16)
    for slot, copy in enumerate(copies):
        copy.wait()
        piece = jnp.transpose(held[slot].astype(f32), (1, 0, 2))
        for part in range(parts):
            out_ref[:, parts * slot + part] = piece[:, part * height : (part + 1) * height].astype(bf16)
    more[1].wait()
    wide_ref[...] = jnp.concatenate([step_ref[...], step_ref[...]], axis=1)
    more[2].wait()
    own_ref[...] = gain_ref[pl.ds(pl.multiple_of(at_ref[0] * stations, stations), stations)]


def dot_nt(left, right):
    return lax.dot_general(left, right, (((1,), (1,)), ((), ())), preferred_element_type=f32)


def weigh(number, both):
    everyone, width = number.shape
    pieces = [
        number == (lanes(number.shape) + (piece * width - 256)).astype(f32)
        for piece in range(everyone // width)
    ]
    chosen = jnp.concatenate([jnp.where(p, 1.0, 0.0).astype(exact) for p in pieces], axis=1)
    half = jnp.dot(chosen, both, preferred_element_type=f32).astype(exact)
    picked = dot_nt(half, chosen)
    rows = lax.broadcasted_iota(jnp.int32, picked.shape, 0)
    return jnp.where(rows == lanes(picked.shape), 0.0, picked * (1.0 / 64.0)).astype(bf16)


def energy_of(volts, resps, gains, weight_ref, out_ref, rows):
    everyone, width = gains.shape
    half = width // 2
    low = lanes(gains.shape) < half
    turned = swap(gains)
    straight = jnp.where(low, gains, turned)
    crossed = jnp.where(low, -turned, gains)
    lefts, rights, backs = [], [], []
    for volt, resp in zip(volts, resps):
        applied = (straight * resp + crossed * swap(resp)).astype(bf16)
        applied_float = applied.astype(f32)
        turned_applied = rotate(applied_float).astype(bf16)
        volt_low = volt.astype(bf16)
        lefts.append(jnp.concatenate([volt_low, (-applied_float).astype(bf16)], axis=1))
        rights.append(
            jnp.concatenate(
                [
                    jnp.concatenate([volt_low, applied], axis=1),
                    jnp.concatenate([rotate(volt).astype(bf16), turned_applied], axis=1),
                ],
                axis=0,
            )
        )
        backs.append(jnp.concatenate([applied, turned_applied], axis=0))
    for start in range(0, everyone, rows):
        weight = weight_ref[start : start + rows]
        weight_both = jnp.concatenate([weight, weight], axis=1)
        same = cross = 0.0
        for left, right, back, resp in zip(lefts, rights, backs, resps):
            short = dot_nt(left[start : start + rows], right)
            residual = weight_both * short.astype(bf16)
            hidden = jnp.dot(residual, back, preferred_element_type=f32)
            part = resp[start : start + rows]
            same = same + part * hidden
            cross = cross + part * swap(hidden)
        real = same + swap(same)
        imag = swap(cross) - cross
        out_ref[start : start + rows] = jnp.where(lanes(real.shape) < half, real, imag)


def slabs(data_ref, first, count, parts):
    devices, _, height, width = data_ref.shape
    found = []
    for slot in range(first, first + count):
        pieces = [data_ref[:, parts * slot + part].astype(f32) for part in range(parts)]
        found.append(jnp.concatenate(pieces, axis=1).reshape(devices * parts * height, width))
    return found


def numbers(data_ref, parts):
    devices, slots, height, width = data_ref.shape
    sent = data_ref[:, slots - 1].astype(f32)
    found = jnp.concatenate([sent] * parts, axis=1)
    part = lax.broadcasted_iota(jnp.int32, found.shape, 1) // height
    found = jnp.where(lanes(found.shape) // (width // parts) == part, found, 0.0)
    turn = width // parts
    while turn < width:
        found = found + pltpu.roll(found, turn, 2)
        turn *= 2
    return found.reshape(devices * parts * height, width)


def first_body(bands, parts, rows, data_ref, flag_ref, gain_ref, out_ref, weight_ref, whole_ref):
    flags = flag_ref[...].astype(f32)
    weight_ref[...] = weigh(numbers(data_ref, parts), (flags * flags.T).astype(exact))
    found = slabs(data_ref, 0, 2 * bands, parts)
    for slot, values in enumerate(found):
        whole_ref[slot] = values.astype(bf16)
    energy_of(
        found[:bands],
        found[bands:],
        gain_ref[...],
        weight_ref,
        out_ref,
        rows,
    )


def next_body(bands, rows, total_ref, step_ref, gain_ref, whole_ref, weight_ref, out_ref, scale_ref):
    everyone, width = gain_ref.shape
    gradient = total_ref[...].reshape(everyone, width) * (-4.0 / width)
    square = jnp.sum(jnp.sum(gradient * gradient, axis=0, keepdims=True), axis=1, keepdims=True)
    scale = 1.0 / jnp.sqrt(square * (2.0 / (everyone * width)) + 1e-06)
    scale_ref[...] = jnp.broadcast_to(scale, scale_ref.shape)
    gains = gain_ref[...] - step_ref[...] * (gradient * scale)
    found = [whole_ref[slot].astype(f32) for slot in range(2 * bands)]
    energy_of(found[:bands], found[bands:], gains, weight_ref, out_ref, rows)


def sum_body(in_ref, out_ref, grad_ref):
    total = jnp.sum(in_ref[...], axis=0)
    out_ref[...] = jnp.broadcast_to(total[None], out_ref.shape)
    grad_ref[...] = total * (-4.0 / in_ref.shape[2])


def split_out_body(in_ref, out_ref):
    blocks, stations = 2, out_ref.shape[1]
    total = jnp.sum(in_ref[...], axis=0)
    each = out_ref.shape[0] // blocks
    for block in range(blocks):
        piece = total[block * stations : (block + 1) * stations]
        out_ref[block * each : (block + 1) * each] = jnp.broadcast_to(piece[None], (each,) + piece.shape)


def square_body(in_ref, grad_ref, out_ref):
    width = in_ref.shape[2]
    gradient = jnp.sum(in_ref[...], axis=0) * (-4.0 / width)
    grad_ref[...] = gradient
    square = jnp.sum(gradient * gradient, axis=0, keepdims=True)
    out_ref[...] = jnp.broadcast_to(square[None], out_ref.shape)


def last_body(everyone, square_ref, grad_ref, gain_ref, step_ref, before_ref, scale_ref, out_ref, descent_ref):
    width = grad_ref.shape[1]
    square = jnp.sum(jnp.sum(square_ref[...], axis=0), axis=1, keepdims=True)
    descent = grad_ref[...] * (1.0 / jnp.sqrt(square * (2.0 / (everyone * width)) + 1e-06))
    gains = gain_ref[...] - step_ref[...] * (before_ref[...] * scale_ref[...])
    descent_ref[...] = descent
    out_ref[...] = gains - step_ref[...] * descent


def shards(voltages, response, start_gains, step_sizes, station_ids, baseline_flags):
    stations, bands, times, width = voltages.shape
    stn = ("plane", "pair")
    plane = lax.axis_size("plane")
    ring = lax.axis_size(stn)
    column = lax.axis_size(("pair", "chan"))
    everyone = stations * ring
    rows = 256
    parts = 4
    shape = jax.ShapeDtypeStruct
    step = step_sizes[None, :]
    at = lax.axis_index(stn).reshape(1)

    def swap_over(values, axis):
        return lax.all_to_all(values, axis, split_axis=0, concat_axis=0, tiled=True)

    sources = (station_ids, voltages, response, start_gains, step)
    packed, own, wide, held = call(
        pack_body,
        (
            shape((ring, 2 * bands * parts + 1, stations // parts, width), bf16),
            shape((stations, width), f32),
            shape((1, width), f32),
            shape((everyone, width), f32),
        ),
        (at,) + tuple(pltpu.with_memory_space_constraint(a, pltpu.HBM) for a in sources),
        "pack",
        smem=(0,),
        left=tuple(range(1, 6)),
        scratch=(
            pltpu.SMEM((stations,), jnp.int32),
            pltpu.VMEM((2 * bands, stations, times, width), bf16),
            pltpu.VMEM(step.shape, f32),
            pltpu.SemaphoreType.DMA((2 * bands + 3,)),
        ),
    )
    data = swap_over(packed, stn)
    energy, weight, whole = call(
        functools.partial(first_body, bands, parts, rows),
        (
            shape((everyone, width), f32),
            shape((everyone, everyone), bf16),
            shape((2 * bands, everyone, width), bf16),
        ),
        (data, baseline_flags, held),
        "first",
    )

    def reduced(energy):
        parts = swap_over(energy.reshape(plane, everyone // plane, width), "plane")
        copies = call(split_out_body, shape((column, stations, width), f32), (parts,), "split")
        return swap_over(copies, ("pair", "chan"))

    copies, before = call(
        sum_body,
        (shape((ring, stations, width), f32), shape((stations, width), f32)),
        (reduced(energy),),
        "sum",
    )
    total = swap_over(copies, stn)
    energy, scale = call(
        functools.partial(next_body, bands, rows),
        (shape((everyone, width), f32), shape((1, width), f32)),
        (total, wide, held, whole, weight),
        "next",
    )
    gradient, square = call(
        square_body,
        (shape((stations, width), f32), shape((ring, 1, width), f32)),
        (reduced(energy),),
        "square",
    )
    squares = swap_over(square, stn)
    return call(
        functools.partial(last_body, everyone),
        (shape((stations, width), f32), shape((stations, width), f32)),
        (squares, gradient, own, wide, before, scale),
        "last",
    )


def solution(mesh):
    pair = 2
    devices = mesh.devices
    finer = Mesh(
        devices.reshape(devices.shape[0] // pair, pair, devices.shape[1]), ("plane", "pair", "chan")
    )
    stn = ("plane", "pair")
    placed = (P(stn, "chan", None, None), P(stn, "chan", None, None), P(), P(), P(stn), P())
    return jax.shard_map(
        shards,
        mesh=finer,
        in_specs=placed,
        out_specs=(P(stn, None), P(stn, None)),
        check_vma=False,
    )
```

```python
import functools

import jax
import jax.numpy as jnp
from jax import lax
from jax.experimental import pallas as pl
from jax.experimental.pallas import tpu as pltpu
from jax.sharding import Mesh
from jax.sharding import PartitionSpec as P

LIMIT = 48 * 1024 * 1024
f32 = jnp.float32
bf16 = jnp.bfloat16
exact = jnp.float8_e4m3fn


def call(body, outs, args, name, smem=(), left=(), scratch=()):
    specs = [
        pl.BlockSpec(memory_space=pltpu.SMEM if i in smem else pltpu.HBM if i in left else pltpu.VMEM)
        for i in range(len(args))
    ]
    single = not isinstance(outs, (tuple, list))
    listed = [outs] if single else list(outs)
    result = pl.pallas_call(
        body,
        out_shape=listed,
        in_specs=specs,
        out_specs=[pl.BlockSpec(memory_space=pltpu.VMEM) for _ in listed],
        scratch_shapes=list(scratch),
        compiler_params=pltpu.CompilerParams(vmem_limit_bytes=LIMIT),
        name=name,
    )(*args)
    return result[0] if single else result


def lanes(shape):
    return lax.broadcasted_iota(jnp.int32, shape, len(shape) - 1)


def swap(values):
    half = values.shape[-1] // 2
    return pltpu.roll(values, half, values.ndim - 1)


def rotate(values):
    half = values.shape[-1] // 2
    turned = swap(values)
    return jnp.where(lanes(values.shape) < half, -turned, turned)


def pack_body(
    at_ref, ids_from, volt_from, resp_from, gain_from, step_from,
    out_ref, own_ref, wide_ref, gain_ref,
    ids_ref, held, step_ref, sems,
):
    bands, stations = held.shape[0] // 2, held.shape[1]
    copies = [
        pltpu.make_async_copy(ref.at[:, band], held.at[slot + band], sems.at[slot + band])
        for slot, ref in ((0, volt_from), (bands, resp_from))
        for band in range(bands)
    ]
    more = [
        pltpu.make_async_copy(source, target, sems.at[2 * bands + i])
        for i, (source, target) in enumerate(
            ((ids_from, ids_ref), (step_from, step_ref), (gain_from, gain_ref))
        )
    ]
    for copy in copies + more:
        copy.start()
    more[0].wait()
    height, columns = out_ref.shape[2:]
    parts = stations // height
    row = lax.broadcasted_iota(jnp.int32, (height, columns), 0)
    column = lanes(row.shape) // (columns // parts)
    number = jnp.zeros(row.shape, f32)
    for station in range(stations):
        here = (row == station % height) & (column == station // height)
        number = jnp.where(here, (ids_ref[station] - 256).astype(f32), number)
    out_ref[:, 2 * bands * parts] = jnp.broadcast_to(
        number[None], (out_ref.shape[0],) + row.shape
    ).astype(bf16)
    for slot, copy in enumerate(copies):
        copy.wait()
        for part in range(parts):
            piece = held[slot, part * height : (part + 1) * height].astype(f32)
            out_ref[:, parts * slot + part] = jnp.transpose(piece, (1, 0, 2)).astype(bf16)
    more[1].wait()
    wide_ref[...] = jnp.concatenate([step_ref[...], step_ref[...]], axis=1)
    more[2].wait()
    own_ref[...] = gain_ref[pl.ds(pl.multiple_of(at_ref[0] * stations, stations), stations)]


def dot_nt(left, right):
    return lax.dot_general(left, right, (((1,), (1,)), ((), ())), preferred_element_type=f32)


def weigh(number, both):
    everyone, width = number.shape
    pieces = [
        number == (lanes(number.shape) + (piece * width - 256)).astype(f32)
        for piece in range(everyone // width)
    ]
    chosen = jnp.concatenate([jnp.where(p, 1.0, 0.0).astype(exact) for p in pieces], axis=1)
    half = jnp.dot(chosen, both, preferred_element_type=f32).astype(exact)
    picked = dot_nt(half, chosen)
    rows = lax.broadcasted_iota(jnp.int32, picked.shape, 0)
    return jnp.where(rows == lanes(picked.shape), 0.0, picked * (1.0 / 64.0)).astype(bf16)


def energy_of(volts, resps, gains, weight_ref, out_ref, rows):
    everyone, width = gains.shape
    half = width // 2
    low = lanes(gains.shape) < half
    turned = swap(gains)
    straight = jnp.where(low, gains, turned)
    crossed = jnp.where(low, -turned, gains)
    lefts, rights, backs = [], [], []
    for volt, resp in zip(volts, resps):
        applied = (straight * resp + crossed * swap(resp)).astype(bf16)
        applied_float = applied.astype(f32)
        turned_applied = rotate(applied_float).astype(bf16)
        volt_low = volt.astype(bf16)
        lefts.append(jnp.concatenate([volt_low, (-applied_float).astype(bf16)], axis=1))
        rights.append(
            jnp.concatenate(
                [
                    jnp.concatenate([volt_low, applied], axis=1),
                    jnp.concatenate([rotate(volt).astype(bf16), turned_applied], axis=1),
                ],
                axis=0,
            )
        )
        backs.append(jnp.concatenate([applied, turned_applied], axis=0))
    for start in range(0, everyone, rows):
        weight = weight_ref[start : start + rows]
        weight_both = jnp.concatenate([weight, weight], axis=1)
        same = cross = 0.0
        for left, right, back, resp in zip(lefts, rights, backs, resps):
            short = dot_nt(left[start : start + rows], right)
            residual = weight_both * short.astype(bf16)
            hidden = jnp.dot(residual, back, preferred_element_type=f32)
            part = resp[start : start + rows]
            same = same + part * hidden
            cross = cross + part * swap(hidden)
        real = same + swap(same)
        imag = swap(cross) - cross
        out_ref[start : start + rows] = jnp.where(lanes(real.shape) < half, real, imag)


def slabs(data_ref, first, count, parts):
    devices, _, height, width = data_ref.shape
    found = []
    for slot in range(first, first + count):
        pieces = [data_ref[:, parts * slot + part].astype(f32) for part in range(parts)]
        found.append(jnp.concatenate(pieces, axis=1).reshape(devices * parts * height, width))
    return found


def numbers(data_ref, parts):
    devices, slots, height, width = data_ref.shape
    sent = data_ref[:, slots - 1].astype(f32)
    found = jnp.concatenate([sent] * parts, axis=1)
    part = lax.broadcasted_iota(jnp.int32, found.shape, 1) // height
    found = jnp.where(lanes(found.shape) // (width // parts) == part, found, 0.0)
    turn = width // parts
    while turn < width:
        found = found + pltpu.roll(found, turn, 2)
        turn *= 2
    return found.reshape(devices * parts * height, width)


def first_body(bands, parts, rows, data_ref, flag_ref, gain_ref, out_ref, weight_ref, whole_ref):
    flags = flag_ref[...].astype(f32)
    weight_ref[...] = weigh(numbers(data_ref, parts), (flags * flags.T).astype(exact))
    found = slabs(data_ref, 0, 2 * bands, parts)
    for slot, values in enumerate(found):
        whole_ref[slot] = values.astype(bf16)
    energy_of(
        found[:bands],
        found[bands:],
        gain_ref[...],
        weight_ref,
        out_ref,
        rows,
    )


def next_body(bands, rows, total_ref, step_ref, gain_ref, whole_ref, weight_ref, out_ref, scale_ref):
    everyone, width = gain_ref.shape
    gradient = total_ref[...].reshape(everyone, width) * (-4.0 / width)
    square = jnp.sum(jnp.sum(gradient * gradient, axis=0, keepdims=True), axis=1, keepdims=True)
    scale = 1.0 / jnp.sqrt(square * (2.0 / (everyone * width)) + 1e-06)
    scale_ref[...] = jnp.broadcast_to(scale, scale_ref.shape)
    gains = gain_ref[...] - step_ref[...] * (gradient * scale)
    found = [whole_ref[slot].astype(f32) for slot in range(2 * bands)]
    energy_of(found[:bands], found[bands:], gains, weight_ref, out_ref, rows)


def sum_body(in_ref, out_ref, grad_ref):
    total = jnp.sum(in_ref[...], axis=0)
    out_ref[...] = jnp.broadcast_to(total[None], out_ref.shape)
    grad_ref[...] = total * (-4.0 / in_ref.shape[2])


def split_out_body(in_ref, out_ref):
    blocks, stations = 2, out_ref.shape[1]
    total = jnp.sum(in_ref[...], axis=0)
    each = out_ref.shape[0] // blocks
    for block in range(blocks):
        piece = total[block * stations : (block + 1) * stations]
        out_ref[block * each : (block + 1) * each] = jnp.broadcast_to(piece[None], (each,) + piece.shape)


def square_body(in_ref, grad_ref, out_ref):
    width = in_ref.shape[2]
    gradient = jnp.sum(in_ref[...], axis=0) * (-4.0 / width)
    grad_ref[...] = gradient
    square = jnp.sum(gradient * gradient, axis=0, keepdims=True)
    out_ref[...] = jnp.broadcast_to(square[None], out_ref.shape)


def last_body(everyone, square_ref, grad_ref, gain_ref, step_ref, before_ref, scale_ref, out_ref, descent_ref):
    width = grad_ref.shape[1]
    square = jnp.sum(jnp.sum(square_ref[...], axis=0), axis=1, keepdims=True)
    descent = grad_ref[...] * (1.0 / jnp.sqrt(square * (2.0 / (everyone * width)) + 1e-06))
    gains = gain_ref[...] - step_ref[...] * (before_ref[...] * scale_ref[...])
    descent_ref[...] = descent
    out_ref[...] = gains - step_ref[...] * descent


def shards(voltages, response, start_gains, step_sizes, station_ids, baseline_flags):
    stations, bands, times, width = voltages.shape
    stn = ("plane", "pair")
    plane = lax.axis_size("plane")
    ring = lax.axis_size(stn)
    column = lax.axis_size(("pair", "chan"))
    everyone = stations * ring
    rows = 256
    parts = 4
    shape = jax.ShapeDtypeStruct
    step = step_sizes[None, :]
    at = lax.axis_index(stn).reshape(1)

    def swap_over(values, axis):
        return lax.all_to_all(values, axis, split_axis=0, concat_axis=0, tiled=True)

    sources = (station_ids, voltages, response, start_gains, step)
    packed, own, wide, held = call(
        pack_body,
        (
            shape((ring, 2 * bands * parts + 1, stations // parts, width), bf16),
            shape((stations, width), f32),
            shape((1, width), f32),
            shape((everyone, width), f32),
        ),
        (at,) + tuple(pltpu.with_memory_space_constraint(a, pltpu.HBM) for a in sources),
        "pack",
        smem=(0,),
        left=tuple(range(1, 6)),
        scratch=(
            pltpu.SMEM((stations,), jnp.int32),
            pltpu.VMEM((2 * bands, stations, times, width), bf16),
            pltpu.VMEM(step.shape, f32),
            pltpu.SemaphoreType.DMA((2 * bands + 3,)),
        ),
    )
    data = swap_over(packed, stn)
    energy, weight, whole = call(
        functools.partial(first_body, bands, parts, rows),
        (
            shape((everyone, width), f32),
            shape((everyone, everyone), bf16),
            shape((2 * bands, everyone, width), bf16),
        ),
        (data, baseline_flags, held),
        "first",
    )

    def reduced(energy):
        parts = swap_over(energy.reshape(plane, everyone // plane, width), "plane")
        copies = call(split_out_body, shape((column, stations, width), f32), (parts,), "split")
        return swap_over(copies, ("pair", "chan"))

    copies, before = call(
        sum_body,
        (shape((ring, stations, width), f32), shape((stations, width), f32)),
        (reduced(energy),),
        "sum",
    )
    total = swap_over(copies, stn)
    energy, scale = call(
        functools.partial(next_body, bands, rows),
        (shape((everyone, width), f32), shape((1, width), f32)),
        (total, wide, held, whole, weight),
        "next",
    )
    gradient, square = call(
        square_body,
        (shape((stations, width), f32), shape((ring, 1, width), f32)),
        (reduced(energy),),
        "square",
    )
    squares = swap_over(square, stn)
    return call(
        functools.partial(last_body, everyone),
        (shape((stations, width), f32), shape((stations, width), f32)),
        (squares, gradient, own, wide, before, scale),
        "last",
    )


def solution(mesh):
    pair = 2
    devices = mesh.devices
    finer = Mesh(
        devices.reshape(devices.shape[0] // pair, pair, devices.shape[1]), ("plane", "pair", "chan")
    )
    stn = ("plane", "pair")
    placed = (P(stn, "chan", None, None), P(stn, "chan", None, None), P(), P(), P(stn), P())
    return jax.shard_map(
        shards,
        mesh=finer,
        in_specs=placed,
        out_specs=(P(stn, None), P(stn, None)),
        check_vma=False,
    )
```

```python
import functools

import jax
import jax.numpy as jnp
from jax import lax
from jax.experimental import pallas as pl
from jax.experimental.pallas import tpu as pltpu
from jax.sharding import Mesh
from jax.sharding import PartitionSpec as P

LIMIT = 48 * 1024 * 1024
f32 = jnp.float32
bf16 = jnp.bfloat16
exact = jnp.float8_e4m3fn


def call(body, outs, args, name, smem=(), left=(), scratch=()):
    specs = [
        pl.BlockSpec(memory_space=pltpu.SMEM if i in smem else pltpu.HBM if i in left else pltpu.VMEM)
        for i in range(len(args))
    ]
    single = not isinstance(outs, (tuple, list))
    listed = [outs] if single else list(outs)
    result = pl.pallas_call(
        body,
        out_shape=listed,
        in_specs=specs,
        out_specs=[pl.BlockSpec(memory_space=pltpu.VMEM) for _ in listed],
        scratch_shapes=list(scratch),
        compiler_params=pltpu.CompilerParams(vmem_limit_bytes=LIMIT),
        name=name,
    )(*args)
    return result[0] if single else result


def lanes(shape):
    return lax.broadcasted_iota(jnp.int32, shape, len(shape) - 1)


def swap(values):
    half = values.shape[-1] // 2
    return pltpu.roll(values, half, values.ndim - 1)


def rotate(values):
    half = values.shape[-1] // 2
    turned = swap(values)
    return jnp.where(lanes(values.shape) < half, -turned, turned)


def pack_body(
    at_ref, ids_from, volt_from, resp_from, gain_from, step_from,
    out_ref, own_ref, wide_ref, gain_ref,
    ids_ref, held, step_ref, sems,
):
    bands, stations = held.shape[0] // 2, held.shape[1]
    copies = [
        pltpu.make_async_copy(ref.at[:, band], held.at[slot + band], sems.at[slot + band])
        for slot, ref in ((0, volt_from), (bands, resp_from))
        for band in range(bands)
    ]
    more = [
        pltpu.make_async_copy(source, target, sems.at[2 * bands + i])
        for i, (source, target) in enumerate(
            ((ids_from, ids_ref), (step_from, step_ref), (gain_from, gain_ref))
        )
    ]
    for copy in copies + more:
        copy.start()
    more[0].wait()
    height, columns = out_ref.shape[2:]
    parts = stations // height
    row = lax.broadcasted_iota(jnp.int32, (height, columns), 0)
    column = lanes(row.shape) // (columns // parts)
    number = jnp.zeros(row.shape, f32)
    for station in range(stations):
        here = (row == station % height) & (column == station // height)
        number = jnp.where(here, (ids_ref[station] - 256).astype(f32), number)
    out_ref[:, 2 * bands * parts] = jnp.broadcast_to(
        number[None], (out_ref.shape[0],) + row.shape
    ).astype(bf16)
    for slot, copy in enumerate(copies):
        copy.wait()
        piece = jnp.transpose(held[slot].astype(f32), (1, 0, 2))
        for part in range(parts):
            out_ref[:, parts * slot + part] = piece[:, part * height : (part + 1) * height].astype(bf16)
    more[1].wait()
    wide_ref[...] = jnp.concatenate([step_ref[...], step_ref[...]], axis=1)
    more[2].wait()
    own_ref[...] = gain_ref[pl.ds(pl.multiple_of(at_ref[0] * stations, stations), stations)]


def dot_nt(left, right):
    return lax.dot_general(left, right, (((1,), (1,)), ((), ())), preferred_element_type=f32)


def weigh(number, both):
    everyone, width = number.shape
    pieces = [
        number == (lanes(number.shape) + (piece * width - 256)).astype(f32)
        for piece in range(everyone // width)
    ]
    chosen = jnp.concatenate([jnp.where(p, 1.0, 0.0).astype(exact) for p in pieces], axis=1)
    half = jnp.dot(chosen, both, preferred_element_type=f32).astype(exact)
    picked = dot_nt(half, chosen)
    rows = lax.broadcasted_iota(jnp.int32, picked.shape, 0)
    return jnp.where(rows == lanes(picked.shape), 0.0, picked * (1.0 / 64.0)).astype(bf16)


def energy_of(volts, resps, gains, weight_ref, out_ref, rows):
    everyone, width = gains.shape
    half = width // 2
    low = lanes(gains.shape) < half
    turned = swap(gains)
    straight = jnp.where(low, gains, turned)
    crossed = jnp.where(low, -turned, gains)
    lefts, rights, backs = [], [], []
    for volt, resp in zip(volts, resps):
        applied = (straight * resp + crossed * swap(resp)).astype(bf16)
        applied_float = applied.astype(f32)
        turned_applied = rotate(applied_float).astype(bf16)
        volt_low = volt.astype(bf16)
        lefts.append(jnp.concatenate([volt_low, (-applied_float).astype(bf16)], axis=1))
        rights.append(
            jnp.concatenate(
                [
                    jnp.concatenate([volt_low, applied], axis=1),
                    jnp.concatenate([rotate(volt).astype(bf16), turned_applied], axis=1),
                ],
                axis=0,
            )
        )
        backs.append(jnp.concatenate([applied, turned_applied], axis=0))
    for start in range(0, everyone, rows):
        weight = weight_ref[start : start + rows]
        weight_both = jnp.concatenate([weight, weight], axis=1)
        same = cross = 0.0
        for left, right, back, resp in zip(lefts, rights, backs, resps):
            short = dot_nt(left[start : start + rows], right)
            residual = weight_both * short.astype(bf16)
            hidden = jnp.dot(residual, back, preferred_element_type=f32)
            part = resp[start : start + rows]
            same = same + part * hidden
            cross = cross + part * swap(hidden)
        real = same + swap(same)
        imag = swap(cross) - cross
        out_ref[start : start + rows] = jnp.where(lanes(real.shape) < half, real, imag)


def slabs(data_ref, first, count, parts):
    devices, _, height, width = data_ref.shape
    found = []
    for slot in range(first, first + count):
        pieces = [data_ref[:, parts * slot + part].astype(f32) for part in range(parts)]
        found.append(jnp.concatenate(pieces, axis=1).reshape(devices * parts * height, width))
    return found


def numbers(data_ref, parts):
    devices, slots, height, width = data_ref.shape
    sent = data_ref[:, slots - 1].astype(f32)
    found = jnp.concatenate([sent] * parts, axis=1)
    part = lax.broadcasted_iota(jnp.int32, found.shape, 1) // height
    found = jnp.where(lanes(found.shape) // (width // parts) == part, found, 0.0)
    turn = width // parts
    while turn < width:
        found = found + pltpu.roll(found, turn, 2)
        turn *= 2
    return found.reshape(devices * parts * height, width)


def first_body(bands, parts, rows, data_ref, flag_ref, gain_ref, out_ref, weight_ref, whole_ref):
    flags = flag_ref[...].astype(f32).astype(bf16)
    weight_ref[...] = weigh(numbers(data_ref, parts), (flags * flags.T).astype(exact))
    found = slabs(data_ref, 0, 2 * bands, parts)
    for slot, values in enumerate(found):
        whole_ref[slot] = values.astype(bf16)
    energy_of(
        found[:bands],
        found[bands:],
        gain_ref[...],
        weight_ref,
        out_ref,
        rows,
    )


def next_body(bands, rows, total_ref, step_ref, gain_ref, whole_ref, weight_ref, out_ref, scale_ref):
    everyone, width = gain_ref.shape
    gradient = total_ref[...].reshape(everyone, width) * (-4.0 / width)
    square = jnp.sum(jnp.sum(gradient * gradient, axis=0, keepdims=True), axis=1, keepdims=True)
    scale = 1.0 / jnp.sqrt(square * (2.0 / (everyone * width)) + 1e-06)
    scale_ref[...] = jnp.broadcast_to(scale, scale_ref.shape)
    gains = gain_ref[...] - step_ref[...] * (gradient * scale)
    found = [whole_ref[slot].astype(f32) for slot in range(2 * bands)]
    energy_of(found[:bands], found[bands:], gains, weight_ref, out_ref, rows)


def sum_body(in_ref, out_ref, grad_ref):
    total = jnp.sum(in_ref[...], axis=0)
    out_ref[...] = jnp.broadcast_to(total[None], out_ref.shape)
    grad_ref[...] = total * (-4.0 / in_ref.shape[2])


def split_out_body(in_ref, out_ref):
    blocks, stations = 2, out_ref.shape[1]
    total = jnp.sum(in_ref[...], axis=0)
    each = out_ref.shape[0] // blocks
    for block in range(blocks):
        piece = total[block * stations : (block + 1) * stations]
        out_ref[block * each : (block + 1) * each] = jnp.broadcast_to(piece[None], (each,) + piece.shape)


def square_body(in_ref, grad_ref, out_ref):
    width = in_ref.shape[2]
    gradient = jnp.sum(in_ref[...], axis=0) * (-4.0 / width)
    grad_ref[...] = gradient
    square = jnp.sum(gradient * gradient, axis=0, keepdims=True)
    out_ref[...] = jnp.broadcast_to(square[None], out_ref.shape)


def last_body(everyone, square_ref, grad_ref, gain_ref, step_ref, before_ref, scale_ref, out_ref, descent_ref):
    width = grad_ref.shape[1]
    square = jnp.sum(jnp.sum(square_ref[...], axis=0), axis=1, keepdims=True)
    descent = grad_ref[...] * (1.0 / jnp.sqrt(square * (2.0 / (everyone * width)) + 1e-06))
    gains = gain_ref[...] - step_ref[...] * (before_ref[...] * scale_ref[...])
    descent_ref[...] = descent
    out_ref[...] = gains - step_ref[...] * descent


def shards(voltages, response, start_gains, step_sizes, station_ids, baseline_flags):
    stations, bands, times, width = voltages.shape
    stn = ("plane", "pair")
    plane = lax.axis_size("plane")
    ring = lax.axis_size(stn)
    column = lax.axis_size(("pair", "chan"))
    everyone = stations * ring
    rows = 256
    parts = 4
    shape = jax.ShapeDtypeStruct
    step = step_sizes[None, :]
    at = lax.axis_index(stn).reshape(1)

    def swap_over(values, axis):
        return lax.all_to_all(values, axis, split_axis=0, concat_axis=0, tiled=True)

    sources = (station_ids, voltages, response, start_gains, step)
    packed, own, wide, held = call(
        pack_body,
        (
            shape((ring, 2 * bands * parts + 1, stations // parts, width), bf16),
            shape((stations, width), f32),
            shape((1, width), f32),
            shape((everyone, width), f32),
        ),
        (at,) + tuple(pltpu.with_memory_space_constraint(a, pltpu.HBM) for a in sources),
        "pack",
        smem=(0,),
        left=tuple(range(1, 6)),
        scratch=(
            pltpu.SMEM((stations,), jnp.int32),
            pltpu.VMEM((2 * bands, stations, times, width), bf16),
            pltpu.VMEM(step.shape, f32),
            pltpu.SemaphoreType.DMA((2 * bands + 3,)),
        ),
    )
    data = swap_over(packed, stn)
    energy, weight, whole = call(
        functools.partial(first_body, bands, parts, rows),
        (
            shape((everyone, width), f32),
            shape((everyone, everyone), bf16),
            shape((2 * bands, everyone, width), bf16),
        ),
        (data, baseline_flags, held),
        "first",
    )

    def reduced(energy):
        parts = swap_over(energy.reshape(plane, everyone // plane, width), "plane")
        copies = call(split_out_body, shape((column, stations, width), f32), (parts,), "split")
        return swap_over(copies, ("pair", "chan"))

    copies, before = call(
        sum_body,
        (shape((ring, stations, width), f32), shape((stations, width), f32)),
        (reduced(energy),),
        "sum",
    )
    total = swap_over(copies, stn)
    energy, scale = call(
        functools.partial(next_body, bands, rows),
        (shape((everyone, width), f32), shape((1, width), f32)),
        (total, wide, held, whole, weight),
        "next",
    )
    gradient, square = call(
        square_body,
        (shape((stations, width), f32), shape((ring, 1, width), f32)),
        (reduced(energy),),
        "square",
    )
    squares = swap_over(square, stn)
    return call(
        functools.partial(last_body, everyone),
        (shape((stations, width), f32), shape((stations, width), f32)),
        (squares, gradient, own, wide, before, scale),
        "last",
    )


def solution(mesh):
    pair = 2
    devices = mesh.devices
    finer = Mesh(
        devices.reshape(devices.shape[0] // pair, pair, devices.shape[1]), ("plane", "pair", "chan")
    )
    stn = ("plane", "pair")
    placed = (P(stn, "chan", None, None), P(stn, "chan", None, None), P(), P(), P(stn), P())
    return jax.shard_map(
        shards,
        mesh=finer,
        in_specs=placed,
        out_specs=(P(stn, None), P(stn, None)),
        check_vma=False,
    )
```
